32 devices in a mesh: pipe: 4 (over z), expert: 8 (over y, x, core).
Axes of the slice: x: 2, y: 2, z: 4, core: 2. Of those that a mesh axis runs over, the one named last changes fastest.
Arguments:
- fwd_state: bfloat16 [4, 192, 3584], P('pipe', 'expert'), may hold values from -6 to 6
- bwd_state: bfloat16 [4, 192, 3584], P('pipe', 'expert'), may hold values from -6 to 6
- saved_input: bfloat16 [4, 2, 192, 3584], P('pipe', None, 'expert'), may hold values from -6 to 6
- fwd_route: int32 [4, 2, 192, 1], P('pipe', None, 'expert'), may hold values from 0 to 3; in each aligned block of 24 rows (0 to 23, 24 to 47, ..., all dimensions but the last counted through in order) at most 7 rows name the same one
- bwd_route: int32 [4, 2, 192, 1], P('pipe', None, 'expert'), may hold values from 0 to 3; in each aligned block of 24 rows (0 to 23, 24 to 47, ..., all dimensions but the last counted through in order) at most 7 rows name the same one
- fwd_gate: float32 [4, 2, 192], P('pipe', None, 'expert'), may hold values from 0.3 to 1
- bwd_gate: float32 [4, 2, 192], P('pipe', None, 'expert'), may hold values from 0.3 to 1
- w_gate: bfloat16 [4, 3584, 1024], P('pipe', None, 'expert'), may hold values from -0.09375 to 0.09375
- w_up: bfloat16 [4, 3584, 1024], P('pipe', None, 'expert'), may hold values from -0.09375 to 0.09375
- w_down: bfloat16 [4, 1024, 3584], P('pipe', 'expert'), may hold values from -0.375 to 0.375
- norm_gain: float32 [4, 3584], P('pipe'), may hold values from 0.5 to 1.5
Outputs:
- fwd_out: bfloat16 [4, 192, 3584], P('pipe', 'expert')
- bwd_out: bfloat16 [4, 192, 3584], P('pipe', 'expert')
The draws below stay inside these ranges and needn't reach their ends.
Inputs may be any that keep to these rules, and one draw needn't show every extreme that they name: `fwd_route`: in the rows of one device at one rank and step, no expert is named more than 7 times, and one is named exactly 7 times. `bwd_route`: as for fwd_route.
All inputs are finite; a program needn't handle non-finite values.
Results may differ from the reference program's by a relative error of at most 0.0068.
Values may be sent and summed in bfloat16 or wider, within the bound.
No kernel may reach another device: no remote copies, remote signals or barrier semaphores. Data moves between devices by JAX's collectives and lax.ppermute only.
A program may use at most 64 MiB of HBM per device.

```python
import math
import jax
import jax.numpy as jnp
import numpy as np
from jax import lax

D = 3584
HID_DEV = 128
EXPERTS = 4
HID = 256
TOK = 24
CAP = 7
TICKS = 2
TOKENS = 192
N_PIPE = 4
N_EXPERT = 8


def block_scale(own_key, extent, split, smallest, top_value):
    level = 1.0
    for position, blocks in split:
        steps = jax.random.uniform(jax.random.fold_in(jax.random.fold_in(own_key, 6), position), (blocks,), jnp.float32, smallest / len(split), top_value / len(split))
        level = level * jnp.repeat(jnp.exp(steps), extent[position] // blocks).reshape((-1,) + (1,) * (len(extent) - 1 - position))
    return level


def routed_block(stream_key, own, number, rows, count, top, bound, slope):
    ranking = jax.random.permutation(stream_key, count)
    packed, common = portions_of(count, rows * top, bound, slope, True), portions_of(count, rows * top, bound, slope, False)
    places = jnp.arange(count)

    def named(sizes, turn):
        used = int((sizes > 0).sum())
        fixed = max(1, used // 4)
        moved = fixed + (places - fixed + turn * (used - fixed)) % max(1, count - fixed)
        return jnp.zeros((count,), jnp.int32).at[ranking[jnp.where(places < fixed, places, moved)]].set(jnp.asarray(sizes, jnp.int32))

    sizes = jnp.where(number % 4 == 0, named(packed, number // 4), named(common, number - number // 4 - 1))
    mixed = jax.random.permutation(jax.random.fold_in(own, 3), count)
    donor, taker = mixed[0:count // 2 * 2:2], mixed[1:count // 2 * 2:2]
    slack = jnp.minimum(sizes[donor] - 1, bound - sizes[taker]) // 2
    slack = jnp.where((donor == ranking[0]) | (taker == ranking[0]) | (sizes[taker] == 0), 0, jnp.maximum(slack, 0))
    moved = jax.random.randint(jax.random.fold_in(own, 4), (count // 2,), 0, 1 << 20) % (slack + 1)
    sizes = sizes.at[donor].add(-moved).at[taker].add(moved)
    members = jnp.searchsorted(jnp.cumsum(sizes), jnp.arange(rows * top), side="right").astype(jnp.int32)
    grid = members.reshape(top, rows).T
    grid = grid[jax.random.permutation(jax.random.fold_in(own, 1), rows)]
    turn = jax.random.randint(jax.random.fold_in(own, 2), (rows, 1), 0, top)
    return jnp.take_along_axis(grid, (jnp.arange(top)[None, :] + turn) % top, axis=1)


def portions_of(amount, total, bound, lean, full):
    loads = [(1 << 20) // math.isqrt(rank ** lean) + 1 for rank in range(1, amount + 1)]
    largest = bound if full else min(bound, max(-(-total // amount), total * loads[0] // sum(loads)))
    least = 1 if total - largest >= amount - 1 else 0
    given, spare = [largest] + [least] * (amount - 1), total - largest - least * (amount - 1)
    while spare > 0:
        candidates = [i for i in range(1, amount) if given[i] < largest] or [i for i in range(1, amount) if given[i] < bound]
        whole, budget = sum([loads[i] for i in candidates]), spare
        for i in candidates:
            extra = min(bound - given[i], max(1, budget * loads[i] // whole), spare)
            given[i] = given[i] + extra
            spare = spare - extra
    return np.array(given)


def scatter_about(own_key, extent, scale, reach, cuts=(), kind=jnp.bfloat16):
    values = jax.random.normal(own_key, extent, jnp.float32) * scale
    if len(cuts) > 0:
        values = block_scale(own_key, extent, cuts, -0.22, 0.18) * values
    return jnp.clip(values, min=-reach, max=reach).astype(kind)


def setup_inputs(seed: int = 0) -> dict:
    splits = jax.random.split(jax.random.key(seed), 12)
    fwd_state = scatter_about(splits[0], (N_PIPE, TOKENS, D), 1.0, 6.0, ((0, 4), (1, 8)))
    bwd_state = scatter_about(splits[1], (N_PIPE, TOKENS, D), 1.0, 6.0, ((0, 4), (1, 8)))
    saved_input = scatter_about(splits[2], (N_PIPE, TICKS, TOKENS, D), 1.0, 6.0, ((0, 4), (2, 8)))
    fwd_route_keys = jax.random.split(jax.random.fold_in(splits[3], 1), N_PIPE * TICKS * TOKENS // TOK)
    fwd_route_turns = jax.random.permutation(jax.random.fold_in(splits[3], 3), N_PIPE * TICKS * TOKENS // TOK)
    fwd_route = jax.vmap(lambda own, number: routed_block(jax.random.fold_in(splits[3], 2), own, number, TOK, EXPERTS, 1, CAP, 2))(fwd_route_keys, fwd_route_turns).reshape((N_PIPE, TICKS, TOKENS, 1))
    bwd_route_keys = jax.random.split(jax.random.fold_in(splits[4], 1), N_PIPE * TICKS * TOKENS // TOK)
    bwd_route_turns = jax.random.permutation(jax.random.fold_in(splits[4], 3), N_PIPE * TICKS * TOKENS // TOK)
    bwd_route = jax.vmap(lambda own, number: routed_block(jax.random.fold_in(splits[4], 2), own, number, TOK, EXPERTS, 1, CAP, 2))(bwd_route_keys, bwd_route_turns).reshape((N_PIPE, TICKS, TOKENS, 1))
    fwd_gate = jnp.clip(jnp.exp(math.log(1.0) - 1.2039728 * jax.random.uniform(splits[5], (N_PIPE, TICKS, TOKENS), jnp.float32) ** block_scale(splits[5], (N_PIPE, TICKS, TOKENS), ((0, 4), (2, 8)), -0.2, 0.2)), 0.3, 1.0)
    bwd_gate = jnp.clip(jnp.exp(math.log(1.0) - 1.2039728 * jax.random.uniform(splits[6], (N_PIPE, TICKS, TOKENS), jnp.float32) ** block_scale(splits[6], (N_PIPE, TICKS, TOKENS), ((0, 4), (2, 8)), -0.2, 0.2)), 0.3, 1.0)
    w_gate = scatter_about(splits[7], (N_PIPE, D, EXPERTS * HID), D ** -0.5, 0.09375, ((0, 4), (2, 8)))
    w_up = scatter_about(splits[8], (N_PIPE, D, EXPERTS * HID), D ** -0.5, 0.09375, ((0, 4), (2, 8)))
    w_down = scatter_about(splits[9], (N_PIPE, EXPERTS * HID, D), HID ** -0.5, 0.375, ((0, 4), (1, 8)))
    norm_gain = jnp.clip(1.0 + 0.1 * jax.random.normal(splits[10], (N_PIPE, D), jnp.float32), 0.5, 1.5)
    return dict(fwd_state=fwd_state, bwd_state=bwd_state, saved_input=saved_input, fwd_route=fwd_route, bwd_route=bwd_route, fwd_gate=fwd_gate, bwd_gate=bwd_gate, w_gate=w_gate, w_up=w_up, w_down=w_down, norm_gain=norm_gain)


EPS = 1e-06

def norm_rows(rows, gain):
    raw = rows.astype(jnp.float32)
    scale = jax.lax.rsqrt(lax.optimization_barrier(jnp.mean(raw * raw, axis=-1, keepdims=True)) + EPS)
    return (raw, scale, (raw * scale * gain).astype(jnp.bfloat16))

def slot_index(route):
    hits = (route[:, None] == jnp.arange(EXPERTS, dtype=jnp.int32)[None, :]).astype(jnp.int32)
    before = jnp.cumsum(hits, axis=0) - hits
    return (route * CAP + lax.optimization_barrier(jnp.sum(before * hits, axis=1))).astype(jnp.int32)

def place_rows(index, rows):
    return jnp.zeros((EXPERTS * CAP, D), jnp.bfloat16).at[index].set(rows)

def take_rows(table, index):
    return jnp.take(table, index, axis=0)

def scatter_tokens(route, normed):
    index = jax.vmap(slot_index)(route.reshape(N_EXPERT, TOK))
    slots = jax.vmap(place_rows)(index, normed.reshape(N_EXPERT, TOK, D))
    return (index, slots)

def expert_block(slots, expert_id):
    return slots[:, expert_id * CAP:(expert_id + 1) * CAP].reshape(N_EXPERT * CAP, D)

def gather_tokens(outputs, index):
    joined = jnp.stack(outputs, axis=0).reshape(EXPERTS, N_EXPERT, CAP, D)
    joined = jnp.transpose(joined, (1, 0, 2, 3)).reshape(N_EXPERT, EXPERTS * CAP, D)
    return jax.vmap(take_rows)(joined, index).reshape(N_EXPERT * TOK, D)

def layer_forward(rows, route, weight, gate_w, up_w, down_w, gain):
    shards = N_EXPERT // EXPERTS
    raw, scale, normed = norm_rows(rows, gain)
    index, slots = scatter_tokens(route, normed)
    outputs = []
    for expert_id in range(EXPERTS):
        block = expert_block(slots, expert_id)
        low = expert_id * HID
        gated = jnp.dot(block, gate_w[:, low:low + HID], preferred_element_type=jnp.float32)
        upped = jnp.dot(block, up_w[:, low:low + HID], preferred_element_type=jnp.float32)
        hidden = (gated * jax.nn.sigmoid(gated) * upped).astype(jnp.bfloat16)
        total = jnp.zeros((N_EXPERT * CAP, D), jnp.float32)
        for group in range(shards):
            cols = slice(group * HID_DEV, (group + 1) * HID_DEV)
            piece = jnp.dot(hidden[:, cols], down_w[low + group * HID_DEV:low + (group + 1) * HID_DEV], preferred_element_type=jnp.float32)
            total = total + piece.astype(jnp.bfloat16).astype(jnp.float32)
        outputs.append(total)
    moe = gather_tokens(outputs, index)
    return (raw + weight[:, None] * moe).astype(jnp.bfloat16)

def layer_backward(grad, saved, route, weight, gate_w, up_w, down_w, gain):
    shards = N_EXPERT // EXPERTS
    raw, scale, normed = norm_rows(saved, gain)
    scaled = (weight[:, None] * grad.astype(jnp.float32)).astype(jnp.bfloat16)
    index, slots = scatter_tokens(route, normed)
    index_g, grad_slots = scatter_tokens(route, scaled)
    outputs = []
    for expert_id in range(EXPERTS):
        block = expert_block(slots, expert_id)
        grad_block = expert_block(grad_slots, expert_id)
        low = expert_id * HID
        gate_part = gate_w[:, low:low + HID]
        up_part = up_w[:, low:low + HID]
        gated = jnp.dot(block, gate_part, preferred_element_type=jnp.float32)
        upped = jnp.dot(block, up_part, preferred_element_type=jnp.float32)
        dhidden = jnp.dot(grad_block, down_w[low:low + HID].T, preferred_element_type=jnp.float32)
        sigma = jax.nn.sigmoid(gated)
        dgate = (dhidden * upped * sigma * (1.0 + gated * (1.0 - sigma))).astype(jnp.bfloat16)
        dup = (dhidden * gated * sigma).astype(jnp.bfloat16)
        total = jnp.zeros((N_EXPERT * CAP, D), jnp.float32)
        for group in range(shards):
            cols = slice(group * HID_DEV, (group + 1) * HID_DEV)
            piece = jnp.dot(dgate[:, cols], gate_part[:, cols].T, preferred_element_type=jnp.float32)
            piece = piece + jnp.dot(dup[:, cols], up_part[:, cols].T, preferred_element_type=jnp.float32)
            total = total + piece.astype(jnp.bfloat16).astype(jnp.float32)
        outputs.append(total)
    dnorm = gather_tokens(outputs, index)
    weighted = gain * dnorm
    dinput = scale * weighted - raw * scale * scale * scale * lax.optimization_barrier(jnp.mean(raw * weighted, axis=-1, keepdims=True))
    return (grad.astype(jnp.float32) + dinput).astype(jnp.bfloat16)

def reference(fwd_state, bwd_state, saved_input, fwd_route, bwd_route, fwd_gate, bwd_gate, w_gate, w_up, w_down, norm_gain):
    forward = [fwd_state[rank] for rank in range(N_PIPE)]
    backward = [bwd_state[rank] for rank in range(N_PIPE)]
    empty = jnp.zeros((N_EXPERT * TOK, D), jnp.bfloat16)
    new_forward = forward
    new_backward = backward
    for moment in range(TICKS):
        new_forward = [layer_forward(forward[rank], fwd_route[rank, moment, :, 0], fwd_gate[rank, moment], w_gate[rank], w_up[rank], w_down[rank], norm_gain[rank]) for rank in range(N_PIPE)]
        new_backward = [layer_backward(backward[rank], saved_input[rank, moment], bwd_route[rank, moment, :, 0], bwd_gate[rank, moment], w_gate[rank], w_up[rank], w_down[rank], norm_gain[rank]) for rank in range(N_PIPE)]
        if moment + 1 < TICKS:
            forward = [empty] + new_forward[:-1]
            backward = new_backward[1:] + [empty]
    return (jnp.stack(new_forward, axis=0), jnp.stack(new_backward, axis=0))
```

```python
import functools

import jax
import jax.numpy as jnp
from jax import lax
from jax.experimental import pallas as pl
from jax.experimental.pallas import tpu as pltpu
from jax.sharding import PartitionSpec as P

EXPERTS = 4
CAP = 7
EPS = 1e-06


SLOT = -(-CAP // 8) * 8
LANES = 128
F32 = jnp.float32
BF16 = jnp.bfloat16


def call(body, outs, args, name, vmem=16):
    return pl.pallas_call(
        body,
        out_shape=outs,
        name=name,
        compiler_params=pltpu.CompilerParams(vmem_limit_bytes=vmem * 2**20),
    )(*args)


class Plan:
    def __init__(self, width, tokens, hidden):
        self.devices = lax.axis_size("expert")
        self.shards = self.devices // EXPERTS
        self.width = width
        self.tokens = tokens
        self.hidden = hidden
        self.share = width // self.shards
        self.cols = -(-self.share // LANES) * LANES
        self.aligned = self.cols == self.share
        self.piece = self.shards * SLOT
        self.rows = EXPERTS * self.piece
        self.units = self.shards * hidden

    def place(self):
        device = lax.axis_index("expert")
        return device // self.shards, device % self.shards

    def cut(self, ref, core, axis):
        if not self.aligned:
            return ref[...]
        span = pl.ds(pl.multiple_of(core * self.cols, LANES), self.cols)
        return ref[:, span] if axis == 1 else ref[span, :]

    def precut(self, array, axis):
        if self.aligned:
            return array
        _, core = self.place()
        part = lax.dynamic_slice_in_dim(array, core * self.share, self.share, axis)
        pad = [(0, 0), (0, 0)]
        pad[axis] = (0, self.cols - self.share)
        return jnp.pad(part, pad)

    def to_member(self, array, offset):
        pairs = [
            (i, (i // self.shards) * self.shards + ((i % self.shards) ^ offset))
            for i in range(self.devices)
        ]
        return lax.ppermute(array, "expert", pairs)

    def members(self, array):
        return [array] + [self.to_member(array, j) for j in range(1, self.shards)]

    def to_expert(self, array, offset):
        pairs = [
            (i, ((i // self.shards) ^ offset) * self.shards + i % self.shards)
            for i in range(self.devices)
        ]
        return lax.ppermute(array, "expert", pairs)

    def exchange(self, pieces):
        moved = {m: self.to_expert(pieces[m], m) for m in range(EXPERTS - 1, 0, -1)}
        return [pieces[0]] + [moved[m] for m in range(1, EXPERTS)]


def ranks(meta, flipped, line, tokens):
    same = flipped[:tokens, line : line + 1] == meta[line : line + 1, :tokens]
    down = lax.broadcasted_iota(jnp.int32, (tokens, tokens), 0)
    across = lax.broadcasted_iota(jnp.int32, (tokens, tokens), 1)
    return same, down, across


def slot_rows(plan, meta, flipped, line, block):
    chip, _ = plan.place()
    same, down, across = ranks(meta, flipped, line, plan.tokens)
    rank = jnp.sum(jnp.where(same & (down < across), 1, 0), axis=0, keepdims=True)
    route = meta[line : line + 1, : plan.tokens].astype(jnp.int32)
    return (route ^ chip) * plan.piece + block * SLOT + rank


def slot_cols(plan, meta, flipped, line, block):
    chip, _ = plan.place()
    same, down, across = ranks(meta, flipped, line, plan.tokens)
    rank = jnp.sum(jnp.where(same & (across < down), 1, 0), axis=1, keepdims=True)
    route = flipped[: plan.tokens, line : line + 1].astype(jnp.int32)
    return (route ^ chip) * plan.piece + block * SLOT + rank


def spread(plan, metas, line, gate_line, blocks):
    _, core = plan.place()
    sums = None
    for j, parts in enumerate(blocks):
        meta = metas[j][...]
        flipped = meta.T
        where = slot_rows(plan, meta, flipped, line, core ^ j)
        down = lax.broadcasted_iota(jnp.int32, (plan.rows, plan.tokens), 0)
        table = jnp.where(down == where, 1.0, 0.0).astype(BF16)
        gate = flipped[: plan.tokens, gate_line : gate_line + 1]
        high = gate.astype(BF16).astype(F32)
        lane = lax.broadcasted_iota(jnp.int32, (plan.tokens, LANES), 1)
        gates = jnp.where(lane == 0, high, jnp.where(lane == 1, gate - high, 0.0)).astype(BF16)
        terms = [
            jnp.dot(table, part, preferred_element_type=F32) for part in [gates] + list(parts)
        ]
        sums = terms if sums is None else [a + b for a, b in zip(sums, terms)]
    return [s.astype(BF16) for s in sums]


def spread_body(plan, line, gate_line, counts, first, *refs):
    _, core = plan.place()
    metas, refs = refs[: plan.shards], refs[plan.shards :]
    kinds = []
    for whole in counts:
        if whole:
            ref, refs = refs[0], refs[1:]
            kinds.append(
                [ref[j * plan.tokens : (j + 1) * plan.tokens, :] for j in range(plan.shards)]
            )
        else:
            group, refs = refs[: plan.shards], refs[plan.shards :]
            kinds.append([plan.cut(r, core, 1) for r in group])
    blocks = [[kind[j] for kind in kinds] for j in range(plan.shards)]
    made = spread(plan, metas, line, gate_line, blocks)
    for m, out in enumerate(refs):
        rows = slice(m * plan.piece, (m + 1) * plan.piece)
        at = 0
        for array in made:
            out[:, at : at + array.shape[1]] = array[rows]
            at += array.shape[1]


def spread_call(plan, metas, line, gate_line, kinds, name):
    args = list(metas)
    counts = []
    for kind in kinds:
        counts.append(not isinstance(kind, list))
        args += kind if isinstance(kind, list) else [kind]
    width = LANES + len(kinds) * plan.cols
    outs = [jax.ShapeDtypeStruct((plan.piece, width), BF16)] * EXPERTS
    body = functools.partial(spread_body, plan, line, gate_line, tuple(counts), True)
    return call(body, outs, args, name)


def gather_body(plan, line, split, *refs):
    metas, refs = refs[: plan.shards], refs[plan.shards :]
    pieces, outs = refs[:EXPERTS], refs[EXPERTS:]
    _, core = plan.place()
    rows = jnp.concatenate([p[...] for p in pieces], axis=0)
    for j in range(plan.shards):
        meta = metas[j][...]
        where = slot_cols(plan, meta, meta.T, line, core ^ j)
        across = lax.broadcasted_iota(jnp.int32, (plan.tokens, plan.rows), 1)
        table = jnp.where(across == where, 1.0, 0.0).astype(BF16)
        picked = jnp.dot(table, rows, preferred_element_type=F32).astype(BF16)
        if split:
            outs[j][...] = picked
        else:
            outs[0][j * plan.tokens : (j + 1) * plan.tokens, :] = picked


def gather_call(plan, metas, line, pieces, split, name):
    if split:
        outs = [jax.ShapeDtypeStruct((plan.tokens, plan.cols), BF16)] * plan.shards
    else:
        outs = jax.ShapeDtypeStruct((plan.shards * plan.tokens, plan.cols), BF16)
    return call(
        functools.partial(gather_body, plan, line, split), outs, list(metas) + list(pieces), name
    )


def pack_body(plan, *refs):
    _, core = plan.place()
    s, h = plan.shards, plan.hidden
    gates, ups, downs = refs[:s], refs[s : 2 * s], refs[2 * s : 3 * s]
    cols_out, rows_out = refs[3 * s :]
    for j in range(s):
        group = core ^ j
        cols_out[:, pl.ds(pl.multiple_of(group * h, h), h)] = plan.cut(gates[j], core, 0)
        cols_out[:, pl.ds(pl.multiple_of(plan.units + group * h, h), h)] = plan.cut(
            ups[j], core, 0
        )
        rows_out[pl.ds(pl.multiple_of(group * h, h), h), :] = plan.cut(downs[j], core, 1)


def scaled_rows(plan, raw, gain_ref):
    _, core = plan.place()
    gain = plan.cut(gain_ref, core, 1)
    values = raw.astype(F32)
    return (values * gain).astype(BF16), jnp.sum(values * values, axis=-1, keepdims=True)


def fwd_in_body(plan, gain_ref, cols_ref, *refs):
    pieces, out = refs[:EXPERTS], refs[EXPERTS]
    rows = jnp.concatenate([p[:, LANES:] for p in pieces], axis=0)
    normed, squares = scaled_rows(plan, rows, gain_ref)
    out[:, : 2 * plan.units] = jnp.dot(normed, cols_ref[...], preferred_element_type=F32)
    out[:, 2 * plan.units :] = jnp.broadcast_to(squares, (plan.rows, LANES))


def total(refs):
    value = refs[0][...]
    for ref in refs[1:]:
        value = value + ref[...]
    return value


def gate_of(pieces):
    gates = jnp.concatenate([p[:, :LANES] for p in pieces], axis=0).astype(F32)
    return gates[:, 0:1] + gates[:, 1:2]


def put_pieces(plan, outs, value):
    for m, out in enumerate(outs):
        out[...] = value[m * plan.piece : (m + 1) * plan.piece]


def fwd_out_body(plan, rows_ref, *refs):
    s, n = plan.shards, plan.units
    sums = total(refs[:s])
    pieces, outs = refs[s : s + EXPERTS], refs[s + EXPERTS :]
    scale = lax.rsqrt(sums[:, 2 * n : 2 * n + 1] / plan.width + EPS)
    gated = sums[:, :n] * scale
    upped = sums[:, n : 2 * n] * scale
    hidden = (gated * jax.nn.sigmoid(gated) * upped).astype(BF16)
    moe = jnp.dot(hidden, rows_ref[...], preferred_element_type=F32)
    raw = jnp.concatenate([p[:, LANES:] for p in pieces], axis=0).astype(F32)
    put_pieces(plan, outs, (raw + gate_of(pieces) * moe).astype(BF16))


def times_transposed(left, right):
    return lax.dot_general(left, right, (((1,), (1,)), ((), ())), preferred_element_type=F32)


def bwd_in_body(plan, gain_ref, cols_ref, rows_ref, *refs):
    pieces, out = refs[:EXPERTS], refs[EXPERTS]
    n = plan.units
    saved = jnp.concatenate([p[:, LANES : LANES + plan.cols] for p in pieces], axis=0)
    grads = jnp.concatenate([p[:, LANES + plan.cols :] for p in pieces], axis=0)
    normed, squares = scaled_rows(plan, saved, gain_ref)
    out[:, : 2 * n] = jnp.dot(normed, cols_ref[...], preferred_element_type=F32)
    out[:, 2 * n : 3 * n] = times_transposed(grads, rows_ref[...])
    out[:, 3 * n :] = jnp.broadcast_to(squares, (plan.rows, LANES))


def bwd_out_body(plan, gain_ref, cols_ref, *refs):
    _, core = plan.place()
    s, n = plan.shards, plan.units
    sums = total(refs[:s])
    pieces, outs = refs[s : s + EXPERTS], refs[s + EXPERTS :]
    scale = lax.rsqrt(sums[:, 3 * n : 3 * n + 1] / plan.width + EPS)
    raw_gated, raw_upped = sums[:, :n], sums[:, n : 2 * n]
    gated, upped = raw_gated * scale, raw_upped * scale
    dhidden = sums[:, 2 * n : 3 * n] * gate_of(pieces)
    sigma = jax.nn.sigmoid(gated)
    dgate = (dhidden * upped * sigma * (1.0 + gated * (1.0 - sigma))).astype(BF16)
    dup = (dhidden * gated * sigma).astype(BF16)
    dnorm = times_transposed(dgate, cols_ref[:, :n]) + times_transposed(dup, cols_ref[:, n:])
    inner = dgate.astype(F32) * raw_gated + dup.astype(F32) * raw_upped
    mean = jnp.sum(inner, axis=-1, keepdims=True) / plan.width
    weighted = plan.cut(gain_ref, core, 1) * dnorm
    saved = jnp.concatenate([p[:, LANES : LANES + plan.cols] for p in pieces], axis=0)
    grads = jnp.concatenate([p[:, LANES + plan.cols :] for p in pieces], axis=0)
    value = grads.astype(F32) + scale * weighted
    value = value - saved.astype(F32) * (scale * scale * scale * mean)
    put_pieces(plan, outs, value.astype(BF16))


def join_body(plan, own, other, out):
    _, core = plan.place()
    size = plan.cols
    out[:, pl.ds(pl.multiple_of(core * size, LANES), size)] = own[...]
    out[:, pl.ds(pl.multiple_of((1 - core) * size, LANES), size)] = other[...]


def join(plan, parts, name):
    if plan.aligned and plan.shards == 2:
        out = jax.ShapeDtypeStruct((plan.tokens, plan.width), BF16)
        return call(functools.partial(join_body, plan), out, parts, name)
    _, core = plan.place()
    order = jnp.arange(plan.shards) ^ core
    stacked = jnp.take(jnp.stack(parts)[:, :, : plan.share], order, axis=0)
    return jnp.transpose(stacked, (1, 0, 2)).reshape(plan.tokens, plan.width)


def shift_states(forward, backward):
    ranks_total = lax.axis_size("pipe")
    even = lax.axis_index("pipe") % 2 == 0

    def swap(array, first):
        pairs = []
        for i in range(first, ranks_total - 1, 2):
            pairs += [(i, i + 1), (i + 1, i)]
        return lax.ppermute(array, "pipe", pairs)

    left = swap(jnp.where(even, forward, backward), 0)
    right = swap(jnp.where(even, backward, forward), 1)
    return jnp.where(even, right, left), jnp.where(even, left, right)


def local(
    fwd_state,
    bwd_state,
    saved_input,
    fwd_route,
    bwd_route,
    fwd_gate,
    bwd_gate,
    w_gate,
    w_up,
    w_down,
    norm_gain,
):
    tokens, width = fwd_state.shape[1:]
    plan = Plan(width, tokens, w_gate.shape[2])
    steps = fwd_route.shape[1]
    lines = jnp.concatenate(
        [
            fwd_route[0, :, :, 0].astype(F32),
            bwd_route[0, :, :, 0].astype(F32),
            fwd_gate[0],
            bwd_gate[0],
        ],
        axis=0,
    )
    lines = jnp.pad(lines, ((0, -lines.shape[0] % 8), (0, LANES - tokens)))
    states = plan.members(fwd_state[0])
    metas = plan.members(lines)
    grads = plan.members(bwd_state[0])
    saved_all = plan.members(saved_input[0].reshape(steps * tokens, width))
    gate_parts = plan.members(w_gate[0])
    up_parts = plan.members(w_up[0])
    down_parts = plan.members(w_down[0])

    gain = plan.precut(norm_gain, 1)
    forward = [plan.precut(a, 1) for a in states]
    backward = [plan.precut(a, 1) for a in grads]
    saved_cut = [plan.precut(a, 1) for a in saved_all]
    weights = [plan.precut(a, 0) for a in gate_parts + up_parts]
    weights += [plan.precut(a, 1) for a in down_parts]
    cols, rows = call(
        functools.partial(pack_body, plan),
        [
            jax.ShapeDtypeStruct((plan.cols, 2 * plan.units), BF16),
            jax.ShapeDtypeStruct((plan.units, plan.cols), BF16),
        ],
        weights,
        "pack",
    )
    piece = jax.ShapeDtypeStruct((plan.piece, plan.cols), BF16)
    for step in range(steps):
        saved = [a[step * tokens : (step + 1) * tokens] for a in saved_cut]
        sent = spread_call(plan, metas, step, 2 * steps + step, [forward], f"fwd_spread_{step}")
        fwd_rows = plan.exchange(sent)
        sent = spread_call(
            plan, metas, steps + step, 3 * steps + step, [saved, backward], f"bwd_spread_{step}"
        )
        bwd_rows = plan.exchange(sent)

        part = call(
            functools.partial(fwd_in_body, plan),
            jax.ShapeDtypeStruct((plan.rows, 2 * plan.units + LANES), F32),
            [gain, cols, *fwd_rows],
            f"fwd_in_{step}",
        )
        back = call(
            functools.partial(fwd_out_body, plan),
            [piece] * EXPERTS,
            [rows, *plan.members(part), *fwd_rows],
            f"fwd_out_{step}",
        )
        fwd_back = plan.exchange(back)

        part = call(
            functools.partial(bwd_in_body, plan),
            jax.ShapeDtypeStruct((plan.rows, 3 * plan.units + LANES), F32),
            [gain, cols, rows, *bwd_rows],
            f"bwd_in_{step}",
        )
        back = call(
            functools.partial(bwd_out_body, plan),
            [piece] * EXPERTS,
            [gain, cols, *plan.members(part), *bwd_rows],
            f"bwd_out_{step}",
        )
        bwd_back = plan.exchange(back)

        last = step + 1 == steps
        forward = gather_call(plan, metas, step, fwd_back, last, f"fwd_gather_{step}")
        backward = gather_call(plan, metas, steps + step, bwd_back, last, f"bwd_gather_{step}")
        if not last:
            forward, backward = shift_states(forward, backward)
    result = []
    for parts, name in ((forward, "fwd_join"), (backward, "bwd_join")):
        parts = [parts[0]] + [plan.to_member(parts[j], j) for j in range(1, plan.shards)]
        result.append(join(plan, parts, name)[None])
    return tuple(result)


def solution(mesh):
    placed = (
        P("pipe", "expert", None),
        P("pipe", "expert", None),
        P("pipe", None, "expert", None),
        P("pipe", None, "expert", None),
        P("pipe", None, "expert", None),
        P("pipe", None, "expert"),
        P("pipe", None, "expert"),
        P("pipe", None, "expert"),
        P("pipe", None, "expert"),
        P("pipe", "expert", None),
        P("pipe", None),
    )
    return jax.shard_map(
        local,
        mesh=mesh,
        in_specs=placed,
        out_specs=(P("pipe", "expert", None), P("pipe", "expert", None)),
        check_vma=False,
    )
```

```python
import functools

import jax
import jax.numpy as jnp
from jax import lax
from jax.experimental import pallas as pl
from jax.experimental.pallas import tpu as pltpu
from jax.sharding import PartitionSpec as P

EXPERTS = 4
CAP = 7
EPS = 1e-06


SLOT = -(-CAP // 8) * 8
LANES = 128
F32 = jnp.float32
BF16 = jnp.bfloat16


def call(body, outs, args, name, vmem=16, **more):
    return pl.pallas_call(
        body,
        out_shape=outs,
        name=name,
        **more,
        compiler_params=pltpu.CompilerParams(vmem_limit_bytes=vmem * 2**20),
    )(*args)


class Plan:
    def __init__(self, width, tokens, hidden):
        self.devices = lax.axis_size("expert")
        self.shards = self.devices // EXPERTS
        self.width = width
        self.tokens = tokens
        self.hidden = hidden
        self.share = width // self.shards
        self.cols = -(-self.share // LANES) * LANES
        self.aligned = self.cols == self.share
        self.piece = self.shards * SLOT
        self.rows = EXPERTS * self.piece
        self.units = self.shards * hidden

    def place(self):
        device = lax.axis_index("expert")
        return device // self.shards, device % self.shards

    def cut(self, ref, core, axis):
        if ref.shape[axis] == self.cols:
            return ref[...]
        span = pl.ds(pl.multiple_of(core * self.cols, LANES), self.cols)
        return ref[:, span] if axis == 1 else ref[span, :]

    def precut(self, array, axis):
        if self.aligned:
            return array
        _, core = self.place()
        part = lax.dynamic_slice_in_dim(array, core * self.share, self.share, axis)
        pad = [(0, 0), (0, 0)]
        pad[axis] = (0, self.cols - self.share)
        return jnp.pad(part, pad)

    def to_member(self, array, offset):
        pairs = [
            (i, (i // self.shards) * self.shards + ((i % self.shards) ^ offset))
            for i in range(self.devices)
        ]
        return lax.ppermute(array, "expert", pairs)

    def others(self, array):
        return [self.to_member(array, j) for j in range(1, self.shards)]

    def members(self, array):
        return [array] + self.others(array)

    def to_expert(self, array, offset):
        pairs = [
            (i, ((i // self.shards) ^ offset) * self.shards + i % self.shards)
            for i in range(self.devices)
        ]
        return lax.ppermute(array, "expert", pairs)

    def exchange(self, pieces):
        moved = {m: self.to_expert(pieces[m], m) for m in range(EXPERTS - 1, 0, -1)}
        return [pieces[0]] + [moved[m] for m in range(1, EXPERTS)]


def ranks(meta, flipped, line, tokens):
    same = flipped[:tokens, line : line + 1] == meta[line : line + 1, :tokens]
    down = lax.broadcasted_iota(jnp.int32, (tokens, tokens), 0)
    across = lax.broadcasted_iota(jnp.int32, (tokens, tokens), 1)
    return same, down, across


def slot_rows(plan, meta, flipped, line, block):
    chip, _ = plan.place()
    same, down, across = ranks(meta, flipped, line, plan.tokens)
    rank = jnp.sum(jnp.where(same & (down < across), 1, 0), axis=0, keepdims=True)
    route = meta[line : line + 1, : plan.tokens].astype(jnp.int32)
    return (route ^ chip) * plan.piece + block * SLOT + rank


def slot_cols(plan, meta, flipped, line, block):
    chip, _ = plan.place()
    same, down, across = ranks(meta, flipped, line, plan.tokens)
    rank = jnp.sum(jnp.where(same & (across < down), 1, 0), axis=1, keepdims=True)
    route = flipped[: plan.tokens, line : line + 1].astype(jnp.int32)
    return (route ^ chip) * plan.piece + block * SLOT + rank


def table_of(plan, metas, j, line):
    _, core = plan.place()
    meta = metas[j][...]
    where = slot_rows(plan, meta, meta.T, line, core ^ j)
    down = lax.broadcasted_iota(jnp.int32, (plan.rows, plan.tokens), 0)
    return jnp.where(down == where, 1.0, 0.0).astype(BF16)


def gate_lanes(plan, metas, j, line, lane):
    gate = metas[j][...].T[: plan.tokens, line : line + 1]
    high = gate.astype(BF16).astype(F32)
    at = lax.broadcasted_iota(jnp.int32, (plan.tokens, LANES), 1) - lane
    return jnp.where(at == 0, high, jnp.where(at == 1, gate - high, 0.0)).astype(BF16)


def moved(tables, parts):
    value = None
    for table, part in zip(tables, parts):
        term = jnp.dot(table, part, preferred_element_type=F32)
        value = term if value is None else value + term
    return value


def spread_body(plan, step, steps, first, *refs):
    _, core = plan.place()
    s, tokens = plan.shards, plan.tokens
    metas, refs = refs[:s], refs[s:]
    if first:
        states, saved, grads, outs = refs[:s], refs[s : 2 * s], refs[2 * s : 3 * s], refs[3 * s :]
        span = slice(step * tokens, (step + 1) * tokens)
        fwd = [plan.cut(r, core, 1) for r in states]
        bwd = [[plan.cut(r.at[span, :], core, 1) for r in saved]]
        bwd += [[plan.cut(r, core, 1) for r in grads]]
    else:
        forward, backward, outs = refs[0], refs[1], refs[2:]
        spans = [slice(j * tokens, (j + 1) * tokens) for j in range(s)]
        fwd = [forward[span, :] for span in spans]
        bwd = [[backward[span, :] for span in spans]]
    fwd_tables = [table_of(plan, metas, j, step) for j in range(s)]
    bwd_tables = [table_of(plan, metas, j, steps + step) for j in range(s)]
    fwd_gates = [gate_lanes(plan, metas, j, 2 * steps + step, 0) for j in range(s)]
    bwd_gates = [gate_lanes(plan, metas, j, 3 * steps + step, 2) for j in range(s)]
    made = [moved(fwd_tables, fwd_gates) + moved(bwd_tables, bwd_gates), moved(fwd_tables, fwd)]
    made += [moved(bwd_tables, kind) for kind in bwd]
    at = 0
    for value in made:
        value = value.astype(BF16)
        width = value.shape[1]
        for m, out in enumerate(outs):
            out[:, at : at + width] = value[m * plan.piece : (m + 1) * plan.piece]
        at += width


def spread_saved_body(plan, step, steps, *refs):
    _, core = plan.place()
    s, tokens = plan.shards, plan.tokens
    metas, saved, outs = refs[:s], refs[s : 2 * s], refs[2 * s :]
    span = slice(step * tokens, (step + 1) * tokens)
    tables = [table_of(plan, metas, j, steps + step) for j in range(s)]
    value = moved(tables, [plan.cut(r.at[span, :], core, 1) for r in saved])
    put_pieces(plan, outs, 0, value.astype(BF16))


def gather_body(plan, step, steps, split, *refs):
    metas, refs = refs[: plan.shards], refs[plan.shards :]
    pieces, outs = refs[:EXPERTS], refs[EXPERTS:]
    _, core = plan.place()
    for stream, line in enumerate((step, steps + step)):
        lanes = slice(stream * plan.cols, (stream + 1) * plan.cols)
        rows = jnp.concatenate([p[:, lanes] for p in pieces], axis=0)
        for j in range(plan.shards):
            meta = metas[j][...]
            where = slot_cols(plan, meta, meta.T, line, core ^ j)
            across = lax.broadcasted_iota(jnp.int32, (plan.tokens, plan.rows), 1)
            table = jnp.where(across == where, 1.0, 0.0).astype(BF16)
            picked = jnp.dot(table, rows, preferred_element_type=F32).astype(BF16)
            if split:
                outs[j][:, lanes] = picked
            else:
                outs[stream][j * plan.tokens : (j + 1) * plan.tokens, :] = picked


def gather_call(plan, metas, step, steps, pieces, split):
    if split:
        outs = [jax.ShapeDtypeStruct((plan.tokens, 2 * plan.cols), BF16)] * plan.shards
    else:
        outs = [jax.ShapeDtypeStruct((plan.shards * plan.tokens, plan.cols), BF16)] * 2
    body = functools.partial(gather_body, plan, step, steps, split)
    return call(body, outs, list(metas) + list(pieces), f"gather_{step}")


def stage_body(plan, *refs):
    _, core = plan.place()
    small, wide, refs = refs[:4], refs[4:7], refs[7:]
    lines, held, scratch, sems = refs[0], refs[1:4], refs[4:8], refs[8]
    copies = [
        pltpu.make_async_copy(src, dst, sems.at[i])
        for i, (src, dst) in enumerate(zip(small, scratch))
    ]
    for i, (src, dst) in enumerate(zip(wide, held)):
        if plan.aligned:
            src = src.at[:, pl.ds(pl.multiple_of(core * plan.cols, LANES), plan.cols)]
        copies.append(pltpu.make_async_copy(src, dst, sems.at[len(small) + i]))
    for copy in copies:
        copy.start()
    lines[...] = jnp.zeros(lines.shape, F32)
    for copy in copies:
        copy.wait()
    for i, ref in enumerate(scratch):
        steps, tokens = ref.shape
        lines[i * steps : (i + 1) * steps, :tokens] = ref[...].astype(F32)


def stage(plan, small, wide):
    steps, tokens = small[0].shape
    outs = [jax.ShapeDtypeStruct((-(-4 * steps // 8) * 8, LANES), F32)]
    outs += [jax.ShapeDtypeStruct((a.shape[0], plan.cols), BF16) for a in wide]
    return call(
        functools.partial(stage_body, plan),
        outs,
        [pltpu.with_memory_space_constraint(a, pltpu.HBM) for a in (*small, *wide)],
        "stage",
        in_specs=[pl.BlockSpec(memory_space=pltpu.HBM)] * (len(small) + len(wide)),
        scratch_shapes=[pltpu.VMEM((steps, tokens), a.dtype) for a in small]
        + [pltpu.SemaphoreType.DMA((len(small) + len(wide),))],
    )


def pack_body(plan, *refs):
    _, core = plan.place()
    s, h = plan.shards, plan.hidden
    gates, ups, downs = refs[:s], refs[s : 2 * s], refs[2 * s : 3 * s]
    cols_out, rows_out = refs[3 * s :]
    for j in range(s):
        group = core ^ j
        cols_out[:, pl.ds(pl.multiple_of(group * h, h), h)] = plan.cut(gates[j], core, 0)
        cols_out[:, pl.ds(pl.multiple_of(plan.units + group * h, h), h)] = plan.cut(
            ups[j], core, 0
        )
        rows_out[pl.ds(pl.multiple_of(group * h, h), h), :] = plan.cut(downs[j], core, 1)


def scaled_rows(plan, raw, gain_ref):
    _, core = plan.place()
    gain = plan.cut(gain_ref, core, 1)
    values = raw.astype(F32)
    return (values * gain).astype(BF16), jnp.sum(values * values, axis=-1, keepdims=True)


def total(refs):
    value = refs[0][...]
    for ref in refs[1:]:
        value = value + ref[...]
    return value


def put_pieces(plan, outs, at, value):
    for m, out in enumerate(outs):
        out[:, at : at + value.shape[1]] = value[m * plan.piece : (m + 1) * plan.piece]


def times_transposed(left, right):
    return lax.dot_general(left, right, (((1,), (1,)), ((), ())), preferred_element_type=F32)


def streams_of(plan, refs, first):
    pieces, refs = refs[:EXPERTS], refs[EXPERTS:]
    w = plan.cols

    def lanes(group, at, width):
        return jnp.concatenate([p[:, at : at + width] for p in group], axis=0)

    gates = lanes(pieces, 0, LANES).astype(F32)
    fwd = lanes(pieces, LANES, w)
    if first:
        return gates, fwd, lanes(pieces, LANES + w, w), lanes(pieces, LANES + 2 * w, w), refs
    group, refs = refs[:EXPERTS], refs[EXPERTS:]
    return gates, fwd, lanes(group, 0, w), lanes(pieces, LANES + w, w), refs


def in_body(plan, first, gain_ref, cols_ref, rows_ref, *refs):
    n = plan.units
    _, fwd, saved, grads, refs = streams_of(plan, refs, first)
    (out,) = refs
    fwd_normed, fwd_squares = scaled_rows(plan, fwd, gain_ref)
    out[:, : 2 * n] = jnp.dot(fwd_normed, cols_ref[...], preferred_element_type=F32)
    bwd_normed, bwd_squares = scaled_rows(plan, saved, gain_ref)
    out[:, 2 * n : 4 * n] = jnp.dot(bwd_normed, cols_ref[...], preferred_element_type=F32)
    out[:, 4 * n : 5 * n] = times_transposed(grads, rows_ref[...])
    lane = lax.broadcasted_iota(jnp.int32, (plan.rows, LANES), 1)
    out[:, 5 * n :] = jnp.where(lane == 0, fwd_squares, bwd_squares)


def out_body(plan, first, gain_ref, cols_ref, rows_ref, *refs):
    _, core = plan.place()
    s, n = plan.shards, plan.units
    sums, refs = refs[:s], refs[s:]
    gates, fwd, saved, grads, outs = streams_of(plan, refs, first)
    value = total(sums)
    scales = lax.rsqrt(value[:, 5 * n :] / plan.width + EPS)

    scale = scales[:, 0:1]
    gated, upped = value[:, :n] * scale, value[:, n : 2 * n] * scale
    hidden = (gated * jax.nn.sigmoid(gated) * upped).astype(BF16)
    moe = jnp.dot(hidden, rows_ref[...], preferred_element_type=F32)
    gate = gates[:, 0:1] + gates[:, 1:2]
    put_pieces(plan, outs, 0, (fwd.astype(F32) + gate * moe).astype(BF16))

    scale = scales[:, 1:2]
    raw_gated, raw_upped = value[:, 2 * n : 3 * n], value[:, 3 * n : 4 * n]
    gated, upped = raw_gated * scale, raw_upped * scale
    dhidden = value[:, 4 * n : 5 * n] * (gates[:, 2:3] + gates[:, 3:4])
    sigma = jax.nn.sigmoid(gated)
    dgate = (dhidden * upped * sigma * (1.0 + gated * (1.0 - sigma))).astype(BF16)
    dup = (dhidden * gated * sigma).astype(BF16)
    dnorm = times_transposed(dgate, cols_ref[:, :n]) + times_transposed(dup, cols_ref[:, n:])
    inner = dgate.astype(F32) * raw_gated + dup.astype(F32) * raw_upped
    mean = jnp.sum(inner, axis=-1, keepdims=True) / plan.width
    weighted = plan.cut(gain_ref, core, 1) * dnorm
    result = grads.astype(F32) + scale * weighted
    result = result - saved.astype(F32) * (scale * scale * scale * mean)
    put_pieces(plan, outs, plan.cols, result.astype(BF16))


def join_body(plan, own, other, *outs):
    _, core = plan.place()
    size = plan.cols
    for stream, out in enumerate(outs):
        lanes = slice(stream * size, (stream + 1) * size)
        out[:, pl.ds(pl.multiple_of(core * size, LANES), size)] = own[:, lanes]
        out[:, pl.ds(pl.multiple_of((1 - core) * size, LANES), size)] = other[:, lanes]


def join(plan, parts):
    if plan.aligned and plan.shards == 2:
        outs = [jax.ShapeDtypeStruct((plan.tokens, plan.width), BF16)] * 2
        return call(functools.partial(join_body, plan), outs, parts, "join")
    _, core = plan.place()
    order = jnp.arange(plan.shards) ^ core
    stacked = jnp.take(jnp.stack(parts), order, axis=0)
    stacked = stacked.reshape(plan.shards, plan.tokens, 2, plan.cols)[..., : plan.share]
    return [
        jnp.transpose(stacked[:, :, i], (1, 0, 2)).reshape(plan.tokens, plan.width)
        for i in range(2)
    ]


def shift_states(forward, backward):
    ranks_total = lax.axis_size("pipe")
    even = lax.axis_index("pipe") % 2 == 0

    def swap(array, first):
        pairs = []
        for i in range(first, ranks_total - 1, 2):
            pairs += [(i, i + 1), (i + 1, i)]
        return lax.ppermute(array, "pipe", pairs)

    left = swap(jnp.where(even, forward, backward), 0)
    right = swap(jnp.where(even, backward, forward), 1)
    return jnp.where(even, right, left), jnp.where(even, left, right)


def local(
    fwd_state,
    bwd_state,
    saved_input,
    fwd_route,
    bwd_route,
    fwd_gate,
    bwd_gate,
    w_gate,
    w_up,
    w_down,
    norm_gain,
):
    tokens, width = fwd_state.shape[1:]
    plan = Plan(width, tokens, w_gate.shape[2])
    steps = fwd_route.shape[1]
    states, grads = plan.others(fwd_state[0]), plan.others(bwd_state[0])
    saved = plan.others(saved_input[0].reshape(steps * tokens, width))
    small = [a.reshape(steps, tokens) for a in (fwd_route, bwd_route, fwd_gate, bwd_gate)]
    wide = [fwd_state[0], saved_input[0].reshape(steps * tokens, width), bwd_state[0]]
    lines, *held = stage(plan, small, [plan.precut(a, 1) for a in wide])
    metas = [lines] + plan.others(lines)
    gain = plan.precut(norm_gain, 1)
    states, saved, grads = (
        [own] + [plan.precut(a, 1) for a in group]
        for own, group in zip(held, (states, saved, grads))
    )

    wide = [jax.ShapeDtypeStruct((plan.piece, LANES + 3 * plan.cols), BF16)] * EXPERTS
    less = [jax.ShapeDtypeStruct((plan.piece, LANES + 2 * plan.cols), BF16)] * EXPERTS
    both = [jax.ShapeDtypeStruct((plan.piece, 2 * plan.cols), BF16)] * EXPERTS
    one = [jax.ShapeDtypeStruct((plan.piece, plan.cols), BF16)] * EXPERTS
    sums = jax.ShapeDtypeStruct((plan.rows, 5 * plan.units + LANES), F32)

    def spread(step, args):
        body = functools.partial(spread_body, plan, step, steps, step == 0)
        return call(body, less if step else wide, [*metas, *args], f"spread_{step}")

    sent = spread(0, [*states, *saved, *grads])
    sent, own = lax.optimization_barrier((sent, (w_gate[0], w_up[0], w_down[0])))
    later = []
    for step in range(1, steps):
        body = functools.partial(spread_saved_body, plan, step, steps)
        later.append(call(body, one, [*metas, *saved], f"spread_saved_{step}"))
    pieces = plan.exchange(sent)
    gate_parts, up_parts, down_parts = (plan.members(a) for a in own)
    weights = [plan.precut(a, 0) for a in gate_parts + up_parts]
    weights += [plan.precut(a, 1) for a in down_parts]
    cols, rows = call(
        functools.partial(pack_body, plan),
        [
            jax.ShapeDtypeStruct((plan.cols, 2 * plan.units), BF16),
            jax.ShapeDtypeStruct((plan.units, plan.cols), BF16),
        ],
        weights,
        "pack",
    )
    cols, rows, later = lax.optimization_barrier((cols, rows, later))
    for step in range(steps):
        first = step == 0
        part = call(
            functools.partial(in_body, plan, first),
            sums,
            [gain, cols, rows, *pieces],
            f"in_{step}",
        )
        back = call(
            functools.partial(out_body, plan, first),
            both,
            [gain, cols, rows, *plan.members(part), *pieces],
            f"out_{step}",
            out_specs=[pl.BlockSpec(memory_space=pltpu.VMEM)] * EXPERTS,
        )
        back = plan.exchange(back)
        last = step + 1 == steps
        made = gather_call(plan, metas, step, steps, back, last)
        if not last:
            made, ahead = lax.optimization_barrier((made, later[step]))
            made, ahead = lax.optimization_barrier((shift_states(*made), plan.exchange(ahead)))
            pieces = plan.exchange(spread(step + 1, made)) + ahead
    parts = [made[0]] + [plan.to_member(made[j], j) for j in range(1, plan.shards)]
    return tuple(out[None] for out in join(plan, parts))


def solution(mesh):
    placed = (
        P("pipe", "expert", None),
        P("pipe", "expert", None),
        P("pipe", None, "expert", None),
        P("pipe", None, "expert", None),
        P("pipe", None, "expert", None),
        P("pipe", None, "expert"),
        P("pipe", None, "expert"),
        P("pipe", None, "expert"),
        P("pipe", None, "expert"),
        P("pipe", "expert", None),
        P("pipe", None),
    )
    return jax.shard_map(
        local,
        mesh=mesh,
        in_specs=placed,
        out_specs=(P("pipe", "expert", None), P("pipe", "expert", None)),
        check_vma=False,
    )
```

```python
import functools

import jax
import jax.numpy as jnp
from jax import lax
from jax.experimental import pallas as pl
from jax.experimental.pallas import tpu as pltpu
from jax.sharding import PartitionSpec as P

EXPERTS = 4
CAP = 7
EPS = 1e-06


SLOT = -(-CAP // 8) * 8
LANES = 128
F32 = jnp.float32
BF16 = jnp.bfloat16


def call(body, outs, args, vmem=16, **more):
    return pl.pallas_call(
        body,
        out_shape=outs,
        compiler_params=pltpu.CompilerParams(vmem_limit_bytes=vmem * 2**20),
        **more,
    )(*args)


def place():
    device = lax.axis_index("expert")
    return device // 2, device % 2


def swap_cores(array):
    pairs = [(i, i ^ 1) for i in range(lax.axis_size("expert"))]
    return lax.ppermute(array, "expert", pairs)


def exchange(pieces):
    moved = [pieces[0]]
    for m in range(1, EXPERTS):
        pairs = [(i, i ^ (2 * m)) for i in range(lax.axis_size("expert"))]
        moved.append(lax.ppermute(pieces[m], "expert", pairs))
    return moved


def swap_ranks(array, first):
    ranks_total, devices = lax.axis_size("pipe"), lax.axis_size("expert")
    target = [i ^ 2 for i in range(ranks_total * devices)]
    for rank in range(first, ranks_total - 1, 2):
        for i in range(devices):
            a, b = rank * devices + i, (rank + 1) * devices + i
            target[a], target[b] = b, a
    return lax.ppermute(array, ("pipe", "expert"), list(enumerate(target)))


def slot_of(rows, line, tokens, axis):
    chip, _ = place()
    row, col = rows[line : line + 1, :tokens], rows.T[:tokens, line : line + 1]
    down = lax.broadcasted_iota(jnp.int32, (tokens, tokens), 0)
    across = lax.broadcasted_iota(jnp.int32, (tokens, tokens), 1)
    earlier = down < across if axis == 0 else across < down
    rank = jnp.sum(jnp.where((row == col) & earlier, 1, 0), axis=axis, keepdims=True)
    route = (row if axis == 0 else col).astype(jnp.int32)
    return (route ^ chip) * SLOT + rank


def table_to_slots(rows, line, tokens, wanted=True):
    down = lax.broadcasted_iota(jnp.int32, (EXPERTS * SLOT, tokens), 0)
    hit = (down == slot_of(rows, line, tokens, 0)) & wanted
    return jnp.where(hit, 1.0, 0.0).astype(BF16)


def table_to_tokens(rows, line, tokens):
    across = lax.broadcasted_iota(jnp.int32, (tokens, EXPERTS * SLOT), 1)
    return jnp.where(across == slot_of(rows, line, tokens, 1), 1.0, 0.0).astype(BF16)


def gate_lanes(rows, line, tokens, lane):
    gate = rows.T[:tokens, line : line + 1]
    high = gate.astype(BF16).astype(F32)
    at = lax.broadcasted_iota(jnp.int32, (tokens, LANES), 1) - lane
    return jnp.where(at == 0, high, jnp.where(at == 1, gate - high, 0.0)).astype(BF16)


def placed(table, rows):
    return jnp.dot(table, rows, preferred_element_type=F32)


def put_pieces(outs, at, value):
    for m, out in enumerate(outs):
        out[:, at : at + value.shape[1]] = value[m * SLOT : (m + 1) * SLOT].astype(BF16)


def put_gates(rows, step, steps, tokens, fwd_table, bwd_table, outs):
    value = placed(fwd_table, gate_lanes(rows, 2 * steps + step, tokens, 0))
    value = value + placed(bwd_table, gate_lanes(rows, 3 * steps + step, tokens, 2))
    put_pieces(outs, 0, value)


def first_spread_body(steps, tokens, *refs):
    small, (state, grad, saved), refs = refs[:4], refs[4:7], refs[7:]
    lines, outs, scratch, sems = refs[0], refs[1 : 1 + EXPERTS], refs[1 + EXPERTS : -1], refs[-1]
    width = state.shape[1]
    sources = [*small, state, grad, saved.at[pl.ds(0, tokens), :]]
    copies = [
        pltpu.make_async_copy(src, dst, sems.at[i])
        for i, (src, dst) in enumerate(zip(sources, scratch))
    ]
    for copy in copies:
        copy.start()
    lines[...] = jnp.zeros(lines.shape, F32)
    for i in range(4):
        copies[i].wait()
        lines[i * steps : (i + 1) * steps, :tokens] = scratch[i][...].astype(F32)
    rows = lines[...]
    fwd_table = table_to_slots(rows, 0, tokens)
    bwd_table = table_to_slots(rows, steps, tokens)
    put_gates(rows, 0, steps, tokens, fwd_table, bwd_table, outs)
    for i, (table, at) in enumerate(((fwd_table, 0), (bwd_table, 1), (bwd_table, 2))):
        copies[4 + i].wait()
        put_pieces(outs, LANES + at * width, placed(table, scratch[4 + i][...]))


def first_spread(small, state, grad, saved):
    steps, tokens = small[0].shape
    width = state.shape[1]
    outs = [jax.ShapeDtypeStruct((-(-4 * steps // 8) * 8, LANES), F32)]
    outs += [jax.ShapeDtypeStruct((SLOT, LANES + 3 * width), BF16)] * EXPERTS
    args = [*small, state, grad, saved]
    return call(
        functools.partial(first_spread_body, steps, tokens),
        outs,
        [pltpu.with_memory_space_constraint(a, pltpu.HBM) for a in args],
        in_specs=[pl.BlockSpec(memory_space=pltpu.HBM)] * len(args),
        scratch_shapes=[pltpu.VMEM((steps, tokens), a.dtype) for a in small]
        + [pltpu.VMEM((tokens, width), BF16)] * 3
        + [pltpu.SemaphoreType.DMA((len(args),))],
    )


def spread_saved_body(step, steps, tokens, *refs):
    lines, saved, outs = refs[0], refs[1], refs[2:]
    table = table_to_slots(lines[...], steps + step, tokens)
    put_pieces(outs, 0, placed(table, saved[step * tokens : (step + 1) * tokens, :]))


def spread_body(step, steps, tokens, *refs):
    lines, low, high, outs = refs[0], refs[1], refs[2], refs[3:]
    width = low.shape[1]
    rank, last = lax.axis_index("pipe"), lax.axis_size("pipe") - 1
    even = rank % 2 == 0
    rows = lines[...]
    fwd_table = table_to_slots(rows, step, tokens, rank != 0)
    bwd_table = table_to_slots(rows, steps + step, tokens, rank != last)
    put_gates(rows, step, steps, tokens, fwd_table, bwd_table, outs)

    def put(forward, backward):
        put_pieces(outs, LANES, placed(fwd_table, forward[...]))
        put_pieces(outs, LANES + width, placed(bwd_table, backward[...]))

    pl.when(even)(lambda: put(high, low))
    pl.when(jnp.logical_not(even))(lambda: put(low, high))


def gather_body(step, steps, tokens, last, *refs):
    lines, pieces, outs = refs[0], refs[1 : 1 + EXPERTS], refs[1 + EXPERTS :]
    width = outs[0].shape[1]
    rows = lines[...]
    even = lax.axis_index("pipe") % 2 == 0
    for stream, line in enumerate((step, steps + step)):
        lanes = slice(stream * width, (stream + 1) * width)
        slots = jnp.concatenate([p[:, lanes] for p in pieces], axis=0)
        value = placed(table_to_tokens(rows, line, tokens), slots).astype(BF16)
        if last:
            outs[stream][...] = value
            continue

        @pl.when(even)
        def _():
            outs[stream][...] = value

        @pl.when(jnp.logical_not(even))
        def _():
            outs[1 - stream][...] = value


def pack_body(*refs):
    _, core = place()
    own, other, (cols_out, rows_out, cols_flip, rows_flip, sems) = refs[:3], refs[3:6], refs[6:]
    h = own[0].shape[1]

    def targets(j):
        at = pl.multiple_of((core ^ j) * h, h)
        return (
            cols_out.at[:, pl.ds(at, h)],
            cols_out.at[:, pl.ds(pl.multiple_of(2 * h + at, h), h)],
            rows_out.at[pl.ds(at, h), :],
        )

    copies = [
        pltpu.make_async_copy(src, dst, sems.at[i])
        for i, (src, dst) in enumerate(zip(own, targets(0)))
    ]
    for copy in copies:
        copy.start()

    def flip(j):
        at = pl.multiple_of((core ^ j) * h, h)
        gates, ups, downs = targets(j)
        cols_flip[pl.ds(at, h), :] = gates[...].T
        cols_flip[pl.ds(pl.multiple_of(2 * h + at, h), h), :] = ups[...].T
        rows_flip[:, pl.ds(at, h)] = downs[...].T

    for src, dst in zip(other, targets(1)):
        dst[...] = src[...]
    flip(1)
    for copy in copies:
        copy.wait()
    flip(0)


def pack(own):
    width, units = own[0].shape
    others = [swap_cores(array) for array in own]
    own = [pltpu.with_memory_space_constraint(array, pltpu.HBM) for array in own]
    return call(
        pack_body,
        [
            jax.ShapeDtypeStruct((width, 4 * units), BF16),
            jax.ShapeDtypeStruct((2 * units, width), BF16),
            jax.ShapeDtypeStruct((4 * units, width), BF16),
            jax.ShapeDtypeStruct((width, 2 * units), BF16),
        ],
        [*own, *others],
        in_specs=[pl.BlockSpec(memory_space=pltpu.HBM)] * 3
        + [pl.BlockSpec(memory_space=pltpu.VMEM)] * 3,
        scratch_shapes=[pltpu.SemaphoreType.DMA((3,))],
    )


def normed_of(rows, gain_ref):
    values = rows.astype(F32)
    mean = jnp.mean(values * values, axis=-1, keepdims=True)
    scale = lax.rsqrt(mean + EPS)
    return scale, (values * scale * gain_ref[...]).astype(BF16)


def expert_body(gain_ref, cols_ref, rows_ref, cols_flip, rows_flip, *refs):
    pieces, outs = refs[:EXPERTS], refs[len(refs) - EXPERTS :]
    n, width = rows_ref.shape
    half = EXPERTS * SLOT

    def lanes(group, at, size):
        return jnp.concatenate([p[:, at : at + size] for p in group], axis=0)

    gates = lanes(pieces, 0, LANES).astype(F32)
    state = lanes(pieces, LANES, width)
    grad = lanes(pieces, LANES + width, width)
    if len(refs) == 2 * EXPERTS:
        saved = lanes(pieces, LANES + 2 * width, width)
    else:
        saved = lanes(refs[EXPERTS : 2 * EXPERTS], 0, width)
    _, fwd_normed = normed_of(state, gain_ref)
    scale, bwd_normed = normed_of(saved, gain_ref)
    normed = jnp.concatenate([fwd_normed, bwd_normed], axis=0)
    both = jnp.dot(normed, cols_ref[...], preferred_element_type=F32)

    gated, upped = both[:half, :n], both[:half, n:]
    hidden = (gated * jax.nn.sigmoid(gated) * upped).astype(BF16)
    moe = jnp.dot(hidden, rows_ref[...], preferred_element_type=F32)
    put_pieces(outs, 0, state.astype(F32) + (gates[:, 0:1] + gates[:, 1:2]) * moe)

    gated, upped = both[half:, :n], both[half:, n:]
    dhidden = jnp.dot(grad, rows_flip[...], preferred_element_type=F32)
    dhidden = dhidden * (gates[:, 2:3] + gates[:, 3:4])
    sigma = jax.nn.sigmoid(gated)
    dgate = (dhidden * upped * sigma * (1.0 + gated * (1.0 - sigma))).astype(BF16)
    dup = (dhidden * gated * sigma).astype(BF16)
    dnorm = jnp.dot(
        jnp.concatenate([dgate, dup], axis=1), cols_flip[...], preferred_element_type=F32
    )
    inner = dgate.astype(F32) * gated + dup.astype(F32) * upped
    mean = jnp.sum(inner, axis=-1, keepdims=True) / width
    value = grad.astype(F32) + scale * (gain_ref[...] * dnorm)
    put_pieces(outs, width, value - saved.astype(F32) * (scale * scale * mean))


def by_home_core(
    fwd_state,
    bwd_state,
    saved_input,
    fwd_route,
    bwd_route,
    fwd_gate,
    bwd_gate,
    w_gate,
    w_up,
    w_down,
    norm_gain,
):
    tokens, width = fwd_state.shape[1:]
    steps = fwd_route.shape[1]
    saved = saved_input[0].reshape(steps * tokens, width)
    small = [a.reshape(steps, tokens) for a in (fwd_route, bwd_route, fwd_gate, bwd_gate)]
    lines, *made = first_spread(small, fwd_state[0], bwd_state[0], saved)
    made, own = lax.optimization_barrier((made, (w_gate[0], w_up[0], w_down[0])))
    pieces = exchange(made)
    weights = pack(own)
    one = [jax.ShapeDtypeStruct((SLOT, width), BF16)] * EXPERTS
    two = [jax.ShapeDtypeStruct((SLOT, 2 * width), BF16)] * EXPERTS
    main = [jax.ShapeDtypeStruct((SLOT, LANES + 2 * width), BF16)] * EXPERTS
    state = [jax.ShapeDtypeStruct((tokens, width), BF16)] * 2
    later = []
    for step in range(1, steps):
        body = functools.partial(spread_saved_body, step, steps, tokens)
        later.append(call(body, one, [lines, saved]))
    weights, later = lax.optimization_barrier((weights, later))
    for step in range(steps):
        back = call(expert_body, two, [norm_gain, *weights, *pieces])
        last = step + 1 == steps
        back = exchange(back)
        body = functools.partial(gather_body, step, steps, tokens, last)
        made = call(body, state, [lines, *back])
        if last:
            return made[0][None], made[1][None]
        made, ahead = lax.optimization_barrier((made, later[step]))
        high = swap_ranks(made[1], 1)
        low = swap_ranks(made[0], 0)
        ahead = exchange(ahead)
        body = functools.partial(spread_body, step + 1, steps, tokens)
        made = call(body, main, [lines, low, high])
        pieces = exchange(made) + ahead


def passed_along(array, axis, by):
    size = lax.axis_size(axis)
    pairs = [(i, i + by) for i in range(size) if 0 <= i + by < size]
    return lax.ppermute(array, axis, pairs)


def norm_rows(rows, gain):
    raw = rows.astype(jnp.float32)
    scale = lax.rsqrt(jnp.mean(raw * raw, axis=-1, keepdims=True) + EPS)
    return (raw, scale, (raw * scale * gain).astype(jnp.bfloat16))


def slot_index(route):
    hits = (route[:, None] == jnp.arange(EXPERTS, dtype=jnp.int32)[None, :]).astype(jnp.int32)
    before = jnp.cumsum(hits, axis=0) - hits
    return route * CAP + jnp.sum(before * hits, axis=1)


def slot_table(index):
    columns = jnp.arange(EXPERTS * CAP, dtype=jnp.int32)
    return (columns[:, None] == index[None, :]).astype(jnp.bfloat16)


def fill_slots(table, rows, shards):
    picked = jnp.dot(table, rows, preferred_element_type=jnp.float32).astype(jnp.bfloat16)
    return jnp.repeat(picked.reshape(EXPERTS, CAP, rows.shape[1]), shards, axis=0)


def collect_rows(returned, index, shards):
    width = returned.shape[2]
    summed = (
        returned.reshape(EXPERTS, shards, returned.shape[1], width).astype(jnp.float32).sum(axis=1)
    )
    return jnp.take(summed.reshape(EXPERTS * CAP, width), index, axis=0)


def by_all_to_all(
    fwd_state,
    bwd_state,
    saved_input,
    fwd_route,
    bwd_route,
    fwd_gate,
    bwd_gate,
    w_gate,
    w_up,
    w_down,
    norm_gain,
):
    shards = lax.axis_size("expert") // EXPERTS
    gain = norm_gain[0]
    gate_cols = w_gate[0]
    up_cols = w_up[0]
    down_rows = w_down[0]
    steps_total = fwd_route.shape[1]
    forward = fwd_state[0]
    backward = bwd_state[0]
    new_forward = forward
    new_backward = backward
    for moment in range(steps_total):
        fwd_index = slot_index(fwd_route[0, moment, :, 0])
        fwd_raw, _, fwd_norm = norm_rows(forward, gain)
        fwd_slots = fill_slots(slot_table(fwd_index), fwd_norm, shards)
        bwd_index = slot_index(bwd_route[0, moment, :, 0])
        bwd_table = slot_table(bwd_index)
        bwd_raw, bwd_scale, bwd_norm = norm_rows(saved_input[0, moment], gain)
        scaled = (bwd_gate[0, moment][:, None] * backward.astype(jnp.float32)).astype(jnp.bfloat16)
        bwd_inputs = fill_slots(bwd_table, bwd_norm, shards)
        bwd_grads = fill_slots(bwd_table, scaled, shards)
        expert_received = lax.all_to_all(
            fwd_slots, "expert", split_axis=0, concat_axis=0, tiled=True
        )
        expert_gated = jnp.einsum(
            "scd,dh->sch", expert_received, gate_cols, preferred_element_type=jnp.float32
        )
        expert_upped = jnp.einsum(
            "scd,dh->sch", expert_received, up_cols, preferred_element_type=jnp.float32
        )
        hidden = (expert_gated * jax.nn.sigmoid(expert_gated) * expert_upped).astype(jnp.bfloat16)
        fwd_partial = jnp.einsum(
            "sch,hd->scd", hidden, down_rows, preferred_element_type=jnp.float32
        ).astype(jnp.bfloat16)
        fwd_back = lax.all_to_all(fwd_partial, "expert", split_axis=0, concat_axis=0, tiled=True)
        inputs_part = lax.all_to_all(bwd_inputs, "expert", split_axis=0, concat_axis=0, tiled=True)
        grads_part = lax.all_to_all(bwd_grads, "expert", split_axis=0, concat_axis=0, tiled=True)
        gated = jnp.einsum(
            "scd,dh->sch", inputs_part, gate_cols, preferred_element_type=jnp.float32
        )
        upped = jnp.einsum("scd,dh->sch", inputs_part, up_cols, preferred_element_type=jnp.float32)
        dhidden = jnp.einsum(
            "scd,hd->sch", grads_part, down_rows, preferred_element_type=jnp.float32
        )
        sigma = jax.nn.sigmoid(gated)
        dgate = (dhidden * upped * sigma * (1.0 + gated * (1.0 - sigma))).astype(jnp.bfloat16)
        dup = (dhidden * gated * sigma).astype(jnp.bfloat16)
        result = jnp.einsum("sch,dh->scd", dgate, gate_cols, preferred_element_type=jnp.float32)
        result = result + jnp.einsum(
            "sch,dh->scd", dup, up_cols, preferred_element_type=jnp.float32
        )
        bwd_partial = result.astype(jnp.bfloat16)
        bwd_back = lax.all_to_all(bwd_partial, "expert", split_axis=0, concat_axis=0, tiled=True)
        moe_rows = collect_rows(fwd_back, fwd_index, shards)
        new_forward = (fwd_raw + fwd_gate[0, moment][:, None] * moe_rows).astype(jnp.bfloat16)
        dnorm = collect_rows(bwd_back, bwd_index, shards)
        weighted = gain * dnorm
        cubed = bwd_scale * bwd_scale * bwd_scale
        dinput = bwd_scale * weighted - bwd_raw * cubed * jnp.mean(
            bwd_raw * weighted, axis=-1, keepdims=True
        )
        new_backward = (backward.astype(jnp.float32) + dinput).astype(jnp.bfloat16)
        if moment + 1 < steps_total:
            forward = passed_along(new_forward, "pipe", 1)
            backward = passed_along(new_backward, "pipe", -1)
    return (new_forward[None], new_backward[None])


def local(*args):
    if lax.axis_size("expert") == 2 * EXPERTS:
        return by_home_core(*args)
    return by_all_to_all(*args)


def solution(mesh):
    specs = (
        P("pipe", "expert", None),
        P("pipe", "expert", None),
        P("pipe", None, "expert", None),
        P("pipe", None, "expert", None),
        P("pipe", None, "expert", None),
        P("pipe", None, "expert"),
        P("pipe", None, "expert"),
        P("pipe", None, "expert"),
        P("pipe", None, "expert"),
        P("pipe", "expert", None),
        P("pipe", None),
    )
    return jax.shard_map(
        local,
        mesh=mesh,
        in_specs=specs,
        out_specs=(P("pipe", "expert", None), P("pipe", "expert", None)),
        check_vma=False,
    )
```

```python
import functools

import jax
import jax.numpy as jnp
from jax import lax
from jax.experimental import pallas as pl
from jax.experimental.pallas import tpu as pltpu
from jax.sharding import PartitionSpec as P

EXPERTS = 4
CAP = 7
EPS = 1e-06


SLOT = -(-CAP // 8) * 8
LANES = 128
F32 = jnp.float32
BF16 = jnp.bfloat16


def call(body, outs, args, vmem=16, **more):
    return pl.pallas_call(
        body,
        out_shape=outs,
        compiler_params=pltpu.CompilerParams(vmem_limit_bytes=vmem * 2**20),
        **more,
    )(*args)


def place():
    device = lax.axis_index("expert")
    return device // 2, device % 2


def swap_cores(array):
    pairs = [(i, i ^ 1) for i in range(lax.axis_size("expert"))]
    return lax.ppermute(array, "expert", pairs)


def exchange(pieces):
    moved = [pieces[0]]
    for m in range(1, EXPERTS):
        pairs = [(i, i ^ (2 * m)) for i in range(lax.axis_size("expert"))]
        moved.append(lax.ppermute(pieces[m], "expert", pairs))
    return moved


def swap_ranks(array, first):
    ranks_total, devices = lax.axis_size("pipe"), lax.axis_size("expert")
    target = [i ^ 2 for i in range(ranks_total * devices)]
    for rank in range(first, ranks_total - 1, 2):
        for i in range(devices):
            a, b = rank * devices + i, (rank + 1) * devices + i
            target[a], target[b] = b, a
    return lax.ppermute(array, ("pipe", "expert"), list(enumerate(target)))


def slot_hits(routes):
    count, tokens = routes.shape
    chip, _ = place()
    routes = routes.astype(jnp.int32)
    expert = lax.broadcasted_iota(jnp.int32, (EXPERTS, tokens), 0)
    named = [jnp.where(expert == routes[i : i + 1], 1.0, 0.0) for i in range(count)]
    down = lax.broadcasted_iota(jnp.int32, (tokens, tokens), 0)
    across = lax.broadcasted_iota(jnp.int32, (tokens, tokens), 1)
    earlier = jnp.where(down < across, 1.0, 0.0).astype(BF16)
    stacked = jnp.concatenate(named, axis=0)
    before = placed(stacked.astype(BF16), earlier) * stacked
    slot = lax.broadcasted_iota(jnp.int32, (EXPERTS * SLOT, tokens), 0)
    hits = []
    for i in range(count):
        rank = jnp.sum(before[i * EXPERTS : (i + 1) * EXPERTS], axis=0, keepdims=True)
        hits.append(slot == (routes[i : i + 1] ^ chip) * SLOT + rank.astype(jnp.int32))
    return hits


def as_table(hits):
    return jnp.where(hits, 1.0, 0.0)


def slot_gates(fwd_hits, bwd_hits, fwd_gates, bwd_gates):
    lane = lax.broadcasted_iota(jnp.int32, (EXPERTS * SLOT, LANES), 1)
    value = jnp.zeros(lane.shape, F32)
    for i, (hits, gates) in enumerate(((fwd_hits, fwd_gates), (bwd_hits, bwd_gates))):
        gate = jnp.sum(jnp.where(hits, gates, 0.0), axis=1, keepdims=True)
        high = gate.astype(BF16).astype(F32)
        value = jnp.where(lane == 2 * i, high, jnp.where(lane == 2 * i + 1, gate - high, value))
    return value


def placed(table, rows):
    return jnp.dot(table, rows, preferred_element_type=F32)


def put_pieces(outs, at, value):
    for m, out in enumerate(outs):
        out[:, at : at + value.shape[1]] = value[m * SLOT : (m + 1) * SLOT].astype(BF16)


def first_spread_body(steps, tokens, *refs):
    small, (state, grad, saved), refs = refs[:4], refs[4:7], refs[7:]
    lines, outs, scratch, sems = refs[0], refs[1 : 1 + EXPERTS], refs[1 + EXPERTS : -1], refs[-1]
    width = state.shape[1]
    sources = [*small, state, grad, saved.at[pl.ds(0, tokens), :]]
    copies = [
        pltpu.make_async_copy(src, dst, sems.at[i])
        for i, (src, dst) in enumerate(zip(sources, scratch))
    ]
    for copy in copies:
        copy.start()
    lines[...] = jnp.zeros(lines.shape, F32)
    for i in range(4):
        copies[i].wait()
        lines[i * steps : (i + 1) * steps, :tokens] = scratch[i][...].astype(F32)
    routes = jnp.concatenate([scratch[0][0:1], scratch[1][0:1]], axis=0)
    fwd_hits, bwd_hits = slot_hits(routes)
    put_pieces(outs, 0, slot_gates(fwd_hits, bwd_hits, scratch[2][0:1], scratch[3][0:1]))
    fwd_table, bwd_table = as_table(fwd_hits).astype(BF16), as_table(bwd_hits).astype(BF16)
    for i, table in enumerate((fwd_table, bwd_table, bwd_table)):
        copies[4 + i].wait()
        put_pieces(outs, LANES + i * width, placed(table, scratch[4 + i][...]))


def first_spread(small, state, grad, saved):
    steps, tokens = small[0].shape
    width = state.shape[1]
    outs = [jax.ShapeDtypeStruct((-(-4 * steps // 8) * 8, LANES), F32)]
    outs += [jax.ShapeDtypeStruct((SLOT, LANES + 3 * width), BF16)] * EXPERTS
    args = [*small, state, grad, saved]
    return call(
        functools.partial(first_spread_body, steps, tokens),
        outs,
        [pltpu.with_memory_space_constraint(a, pltpu.HBM) for a in args],
        in_specs=[pl.BlockSpec(memory_space=pltpu.HBM)] * len(args),
        scratch_shapes=[pltpu.VMEM((steps, tokens), a.dtype) for a in small]
        + [pltpu.VMEM((tokens, width), BF16)] * 3
        + [pltpu.SemaphoreType.DMA((len(args),))],
    )


def prepare_body(steps, tokens, *refs):
    lines, saved, to_tokens, to_slots, gates, later = *refs[:5], refs[5:]
    rank, last = lax.axis_index("pipe"), lax.axis_size("pipe") - 1
    rows = lines[...]
    across = slice(0, tokens)
    for step in range(steps):
        at = (step, steps + step, 2 * steps + step, 3 * steps + step)
        fwd_row, bwd_row, fwd_gate, bwd_gate = (rows[i : i + 1, across] for i in at)
        hits = slot_hits(jnp.concatenate([fwd_row, bwd_row], axis=0))
        gates[step] = slot_gates(*hits, fwd_gate, bwd_gate).astype(BF16)
        for i, end in enumerate((0, last)):
            table = as_table(hits[i])
            to_tokens[2 * step + i] = table.T.astype(BF16)
            come = as_table(hits[i] & (rank != end)).astype(BF16)
            to_slots[2 * step + i] = come
        if step:
            table = table.astype(BF16)
            outs = later[(step - 1) * EXPERTS : step * EXPERTS]
            put_pieces(outs, 0, placed(table, saved[step * tokens : (step + 1) * tokens, :]))


def prepare(lines, saved, steps, tokens):
    slots = EXPERTS * SLOT
    outs = [
        jax.ShapeDtypeStruct((2 * steps, tokens, slots), BF16),
        jax.ShapeDtypeStruct((2 * steps, slots, tokens), BF16),
        jax.ShapeDtypeStruct((steps, slots, LANES), BF16),
    ]
    outs += [jax.ShapeDtypeStruct((SLOT, saved.shape[1]), BF16)] * (EXPERTS * (steps - 1))
    body = functools.partial(prepare_body, steps, tokens)
    to_tokens, to_slots, gates, *later = call(body, outs, [lines, saved])
    later = [later[i * EXPERTS : (i + 1) * EXPERTS] for i in range(steps - 1)]
    return (to_tokens, to_slots, gates), later


def spread_body(step, tables, gates, low, high, *outs):
    width = low.shape[1]
    even = lax.axis_index("pipe") % 2 == 0
    for m, out in enumerate(outs):
        out[:, :LANES] = gates[step, m * SLOT : (m + 1) * SLOT, :]

    def put(forward, backward):
        put_pieces(outs, LANES, placed(tables[2 * step], forward[...]))
        put_pieces(outs, LANES + width, placed(tables[2 * step + 1], backward[...]))

    pl.when(even)(lambda: put(high, low))
    pl.when(jnp.logical_not(even))(lambda: put(low, high))


def gather_body(step, last, tables, *refs):
    pieces, outs = refs[:EXPERTS], refs[EXPERTS:]
    width = outs[0].shape[1]

    def put(*targets):
        for stream, out in enumerate(targets):
            lanes = slice(stream * width, (stream + 1) * width)
            slots = jnp.concatenate([p[:, lanes] for p in pieces], axis=0)
            out[...] = placed(tables[2 * step + stream], slots).astype(BF16)

    if last:
        put(*outs)
    else:
        even = lax.axis_index("pipe") % 2 == 0
        pl.when(even)(lambda: put(outs[0], outs[1]))
        pl.when(jnp.logical_not(even))(lambda: put(outs[1], outs[0]))


def pack_body(*refs):
    _, core = place()
    own, other, (cols_out, rows_out, cols_flip, rows_flip, sems) = refs[:3], refs[3:6], refs[6:]
    h = own[0].shape[1]

    def targets(j):
        at = pl.multiple_of((core ^ j) * h, h)
        return (
            cols_out.at[:, pl.ds(at, h)],
            cols_out.at[:, pl.ds(pl.multiple_of(2 * h + at, h), h)],
            rows_out.at[pl.ds(at, h), :],
        )

    copies = [
        pltpu.make_async_copy(src, dst, sems.at[i])
        for i, (src, dst) in enumerate(zip(own, targets(0)))
    ]
    for copy in copies:
        copy.start()

    def flip(j):
        at = pl.multiple_of((core ^ j) * h, h)
        gates, ups, downs = targets(j)
        cols_flip[pl.ds(at, h), :] = gates[...].T
        cols_flip[pl.ds(pl.multiple_of(2 * h + at, h), h), :] = ups[...].T
        rows_flip[:, pl.ds(at, h)] = downs[...].T

    for src, dst in zip(other, targets(1)):
        dst[...] = src[...]
    flip(1)
    for copy in copies:
        copy.wait()
    flip(0)


def pack(own):
    width, units = own[0].shape
    others = [swap_cores(array) for array in own]
    own = [pltpu.with_memory_space_constraint(array, pltpu.HBM) for array in own]
    return call(
        pack_body,
        [
            jax.ShapeDtypeStruct((width, 4 * units), BF16),
            jax.ShapeDtypeStruct((2 * units, width), BF16),
            jax.ShapeDtypeStruct((4 * units, width), BF16),
            jax.ShapeDtypeStruct((width, 2 * units), BF16),
        ],
        [*own, *others],
        in_specs=[pl.BlockSpec(memory_space=pltpu.HBM)] * 3
        + [pl.BlockSpec(memory_space=pltpu.VMEM)] * 3,
        scratch_shapes=[pltpu.SemaphoreType.DMA((3,))],
    )


def normed_of(rows, gain_ref):
    values = rows.astype(F32)
    mean = jnp.mean(values * values, axis=-1, keepdims=True)
    scale = lax.rsqrt(mean + EPS)
    return scale, (values * scale * gain_ref[...]).astype(BF16)


def expert_body(gain_ref, cols_ref, rows_ref, cols_flip, rows_flip, *refs):
    pieces, outs = refs[:EXPERTS], refs[len(refs) - EXPERTS :]
    n, width = rows_ref.shape
    half = EXPERTS * SLOT

    def lanes(group, at, size):
        return jnp.concatenate([p[:, at : at + size] for p in group], axis=0)

    gates = lanes(pieces, 0, LANES).astype(F32)
    state = lanes(pieces, LANES, width)
    grad = lanes(pieces, LANES + width, width)
    if len(refs) == 2 * EXPERTS:
        saved = lanes(pieces, LANES + 2 * width, width)
    else:
        saved = lanes(refs[EXPERTS : 2 * EXPERTS], 0, width)
    _, fwd_normed = normed_of(state, gain_ref)
    scale, bwd_normed = normed_of(saved, gain_ref)
    normed = jnp.concatenate([fwd_normed, bwd_normed], axis=0)
    both = jnp.dot(normed, cols_ref[...], preferred_element_type=F32)

    gated, upped = both[:half, :n], both[:half, n:]
    hidden = (gated * jax.nn.sigmoid(gated) * upped).astype(BF16)
    moe = jnp.dot(hidden, rows_ref[...], preferred_element_type=F32)
    put_pieces(outs, 0, state.astype(F32) + (gates[:, 0:1] + gates[:, 1:2]) * moe)

    gated, upped = both[half:, :n], both[half:, n:]
    dhidden = jnp.dot(grad, rows_flip[...], preferred_element_type=F32)
    dhidden = dhidden * (gates[:, 2:3] + gates[:, 3:4])
    sigma = jax.nn.sigmoid(gated)
    dgate = (dhidden * upped * sigma * (1.0 + gated * (1.0 - sigma))).astype(BF16)
    dup = (dhidden * gated * sigma).astype(BF16)
    dnorm = jnp.dot(
        jnp.concatenate([dgate, dup], axis=1), cols_flip[...], preferred_element_type=F32
    )
    inner = dgate.astype(F32) * gated + dup.astype(F32) * upped
    mean = jnp.sum(inner, axis=-1, keepdims=True) / width
    value = grad.astype(F32) + scale * (gain_ref[...] * dnorm)
    put_pieces(outs, width, value - saved.astype(F32) * (scale * scale * mean))


def by_home_core(
    fwd_state,
    bwd_state,
    saved_input,
    fwd_route,
    bwd_route,
    fwd_gate,
    bwd_gate,
    w_gate,
    w_up,
    w_down,
    norm_gain,
):
    tokens, width = fwd_state.shape[1:]
    steps = fwd_route.shape[1]
    saved = saved_input[0].reshape(steps * tokens, width)
    small = [a.reshape(steps, tokens) for a in (fwd_route, bwd_route, fwd_gate, bwd_gate)]
    lines, *made = first_spread(small, fwd_state[0], bwd_state[0], saved)
    made, own = lax.optimization_barrier((made, (w_gate[0], w_up[0], w_down[0])))
    pieces = exchange(made)
    weights = pack(own)
    two = [jax.ShapeDtypeStruct((SLOT, 2 * width), BF16)] * EXPERTS
    main = [jax.ShapeDtypeStruct((SLOT, LANES + 2 * width), BF16)] * EXPERTS
    state = [jax.ShapeDtypeStruct((tokens, width), BF16)] * 2
    tables, later = prepare(lines, saved, steps, tokens)
    weights, tables, later = lax.optimization_barrier((weights, tables, later))
    to_tokens, to_slots, gates = tables
    for step in range(steps):
        back = call(expert_body, two, [norm_gain, *weights, *pieces])
        last = step + 1 == steps
        back = exchange(back)
        body = functools.partial(gather_body, step, last)
        made = call(body, state, [to_tokens, *back])
        if last:
            return made[0][None], made[1][None]
        made, ahead = lax.optimization_barrier((made, later[step]))
        high = swap_ranks(made[1], 1)
        low = swap_ranks(made[0], 0)
        ahead = exchange(ahead)
        body = functools.partial(spread_body, step + 1)
        made = call(body, main, [to_slots, gates, low, high])
        pieces = exchange(made) + ahead


def passed_along(array, axis, by):
    size = lax.axis_size(axis)
    pairs = [(i, i + by) for i in range(size) if 0 <= i + by < size]
    return lax.ppermute(array, axis, pairs)


def norm_rows(rows, gain):
    raw = rows.astype(jnp.float32)
    scale = lax.rsqrt(jnp.mean(raw * raw, axis=-1, keepdims=True) + EPS)
    return (raw, scale, (raw * scale * gain).astype(jnp.bfloat16))


def slot_index(route):
    hits = (route[:, None] == jnp.arange(EXPERTS, dtype=jnp.int32)[None, :]).astype(jnp.int32)
    before = jnp.cumsum(hits, axis=0) - hits
    return route * CAP + jnp.sum(before * hits, axis=1)


def slot_table(index):
    columns = jnp.arange(EXPERTS * CAP, dtype=jnp.int32)
    return (columns[:, None] == index[None, :]).astype(jnp.bfloat16)


def fill_slots(table, rows, shards):
    picked = jnp.dot(table, rows, preferred_element_type=jnp.float32).astype(jnp.bfloat16)
    return jnp.repeat(picked.reshape(EXPERTS, CAP, rows.shape[1]), shards, axis=0)


def collect_rows(returned, index, shards):
    width = returned.shape[2]
    summed = (
        returned.reshape(EXPERTS, shards, returned.shape[1], width).astype(jnp.float32).sum(axis=1)
    )
    return jnp.take(summed.reshape(EXPERTS * CAP, width), index, axis=0)


def by_all_to_all(
    fwd_state,
    bwd_state,
    saved_input,
    fwd_route,
    bwd_route,
    fwd_gate,
    bwd_gate,
    w_gate,
    w_up,
    w_down,
    norm_gain,
):
    shards = lax.axis_size("expert") // EXPERTS
    gain = norm_gain[0]
    gate_cols = w_gate[0]
    up_cols = w_up[0]
    down_rows = w_down[0]
    steps_total = fwd_route.shape[1]
    forward = fwd_state[0]
    backward = bwd_state[0]
    new_forward = forward
    new_backward = backward
    for moment in range(steps_total):
        fwd_index = slot_index(fwd_route[0, moment, :, 0])
        fwd_raw, _, fwd_norm = norm_rows(forward, gain)
        fwd_slots = fill_slots(slot_table(fwd_index), fwd_norm, shards)
        bwd_index = slot_index(bwd_route[0, moment, :, 0])
        bwd_table = slot_table(bwd_index)
        bwd_raw, bwd_scale, bwd_norm = norm_rows(saved_input[0, moment], gain)
        scaled = (bwd_gate[0, moment][:, None] * backward.astype(jnp.float32)).astype(jnp.bfloat16)
        bwd_inputs = fill_slots(bwd_table, bwd_norm, shards)
        bwd_grads = fill_slots(bwd_table, scaled, shards)
        expert_received = lax.all_to_all(
            fwd_slots, "expert", split_axis=0, concat_axis=0, tiled=True
        )
        expert_gated = jnp.einsum(
            "scd,dh->sch", expert_received, gate_cols, preferred_element_type=jnp.float32
        )
        expert_upped = jnp.einsum(
            "scd,dh->sch", expert_received, up_cols, preferred_element_type=jnp.float32
        )
        hidden = (expert_gated * jax.nn.sigmoid(expert_gated) * expert_upped).astype(jnp.bfloat16)
        fwd_partial = jnp.einsum(
            "sch,hd->scd", hidden, down_rows, preferred_element_type=jnp.float32
        ).astype(jnp.bfloat16)
        fwd_back = lax.all_to_all(fwd_partial, "expert", split_axis=0, concat_axis=0, tiled=True)
        inputs_part = lax.all_to_all(bwd_inputs, "expert", split_axis=0, concat_axis=0, tiled=True)
        grads_part = lax.all_to_all(bwd_grads, "expert", split_axis=0, concat_axis=0, tiled=True)
        gated = jnp.einsum(
            "scd,dh->sch", inputs_part, gate_cols, preferred_element_type=jnp.float32
        )
        upped = jnp.einsum("scd,dh->sch", inputs_part, up_cols, preferred_element_type=jnp.float32)
        dhidden = jnp.einsum(
            "scd,hd->sch", grads_part, down_rows, preferred_element_type=jnp.float32
        )
        sigma = jax.nn.sigmoid(gated)
        dgate = (dhidden * upped * sigma * (1.0 + gated * (1.0 - sigma))).astype(jnp.bfloat16)
        dup = (dhidden * gated * sigma).astype(jnp.bfloat16)
        result = jnp.einsum("sch,dh->scd", dgate, gate_cols, preferred_element_type=jnp.float32)
        result = result + jnp.einsum(
            "sch,dh->scd", dup, up_cols, preferred_element_type=jnp.float32
        )
        bwd_partial = result.astype(jnp.bfloat16)
        bwd_back = lax.all_to_all(bwd_partial, "expert", split_axis=0, concat_axis=0, tiled=True)
        moe_rows = collect_rows(fwd_back, fwd_index, shards)
        new_forward = (fwd_raw + fwd_gate[0, moment][:, None] * moe_rows).astype(jnp.bfloat16)
        dnorm = collect_rows(bwd_back, bwd_index, shards)
        weighted = gain * dnorm
        cubed = bwd_scale * bwd_scale * bwd_scale
        dinput = bwd_scale * weighted - bwd_raw * cubed * jnp.mean(
            bwd_raw * weighted, axis=-1, keepdims=True
        )
        new_backward = (backward.astype(jnp.float32) + dinput).astype(jnp.bfloat16)
        if moment + 1 < steps_total:
            forward = passed_along(new_forward, "pipe", 1)
            backward = passed_along(new_backward, "pipe", -1)
    return (new_forward[None], new_backward[None])


def local(*args):
    if lax.axis_size("expert") == 2 * EXPERTS:
        return by_home_core(*args)
    return by_all_to_all(*args)


def solution(mesh):
    specs = (
        P("pipe", "expert", None),
        P("pipe", "expert", None),
        P("pipe", None, "expert", None),
        P("pipe", None, "expert", None),
        P("pipe", None, "expert", None),
        P("pipe", None, "expert"),
        P("pipe", None, "expert"),
        P("pipe", None, "expert"),
        P("pipe", None, "expert"),
        P("pipe", "expert", None),
        P("pipe", None),
    )
    return jax.shard_map(
        local,
        mesh=mesh,
        in_specs=specs,
        out_specs=(P("pipe", "expert", None), P("pipe", "expert", None)),
        check_vma=False,
    )
```

```python
import functools

import jax
import jax.numpy as jnp
from jax import lax
from jax.experimental import pallas as pl
from jax.experimental.pallas import tpu as pltpu
from jax.sharding import PartitionSpec as P

EXPERTS = 4
CAP = 7
EPS = 1e-06


SLOT = -(-CAP // 8) * 8
LANES = 128
F32 = jnp.float32
BF16 = jnp.bfloat16


def call(body, outs, args, vmem=16, **more):
    return pl.pallas_call(
        body,
        out_shape=outs,
        compiler_params=pltpu.CompilerParams(vmem_limit_bytes=vmem * 2**20),
        **more,
    )(*args)


def place():
    device = lax.axis_index("expert")
    return device // 2, device % 2


def swap_cores(array):
    pairs = [(i, i ^ 1) for i in range(lax.axis_size("expert"))]
    return lax.ppermute(array, "expert", pairs)


def exchange(pieces):
    moved = [pieces[0]]
    for m in range(1, EXPERTS):
        pairs = [(i, i ^ (2 * m)) for i in range(lax.axis_size("expert"))]
        moved.append(lax.ppermute(pieces[m], "expert", pairs))
    return moved


def swap_ranks(array, first):
    ranks_total, devices = lax.axis_size("pipe"), lax.axis_size("expert")
    target = [i ^ 1 for i in range(ranks_total * devices)]
    for rank in range(first, ranks_total - 1, 2):
        for i in range(devices):
            a, b = rank * devices + i, (rank + 1) * devices + i
            target[a], target[b] = b, a
    return lax.ppermute(array, ("pipe", "expert"), list(enumerate(target)))


def slot_hits(routes):
    count, tokens = routes.shape
    chip, _ = place()
    routes = routes.astype(jnp.int32)
    expert = lax.broadcasted_iota(jnp.int32, (EXPERTS, tokens), 0)
    named = [jnp.where(expert == routes[i : i + 1], 1.0, 0.0) for i in range(count)]
    down = lax.broadcasted_iota(jnp.int32, (tokens, tokens), 0)
    across = lax.broadcasted_iota(jnp.int32, (tokens, tokens), 1)
    earlier = jnp.where(down < across, 1.0, 0.0).astype(BF16)
    stacked = jnp.concatenate(named, axis=0)
    before = placed(stacked.astype(BF16), earlier) * stacked
    slot = lax.broadcasted_iota(jnp.int32, (EXPERTS * SLOT, tokens), 0)
    hits = []
    for i in range(count):
        rank = jnp.sum(before[i * EXPERTS : (i + 1) * EXPERTS], axis=0, keepdims=True)
        hits.append(slot == (routes[i : i + 1] ^ chip) * SLOT + rank.astype(jnp.int32))
    return hits


def as_table(hits):
    return jnp.where(hits, 1.0, 0.0)


def slot_gates(fwd_hits, bwd_hits, fwd_gates, bwd_gates):
    lane = lax.broadcasted_iota(jnp.int32, (EXPERTS * SLOT, LANES), 1)
    value = jnp.zeros(lane.shape, F32)
    for i, (hits, gates) in enumerate(((fwd_hits, fwd_gates), (bwd_hits, bwd_gates))):
        gate = jnp.sum(jnp.where(hits, gates, 0.0), axis=1, keepdims=True)
        high = gate.astype(BF16).astype(F32)
        value = jnp.where(lane == 2 * i, high, jnp.where(lane == 2 * i + 1, gate - high, value))
    return value


def placed(table, rows):
    return jnp.dot(table, rows, preferred_element_type=F32)


def put_pieces(outs, at, value):
    for m, out in enumerate(outs):
        out[:, at : at + value.shape[1]] = value[m * SLOT : (m + 1) * SLOT].astype(BF16)


def folded(width):
    if SLOT == CAP:
        return width, 0
    tail = width // LANES // (CAP + 1) * LANES
    return width - tail, tail


def put_folded(outs, at, parts):
    head, tail = folded(sum(p.shape[1] for p in parts))
    down = lax.broadcasted_iota(jnp.int32, (SLOT, head), 0)
    for m, out in enumerate(outs):
        rows = jnp.concatenate([p[m * SLOT : (m + 1) * SLOT] for p in parts], axis=1)
        value = rows[:, :head]
        if tail:
            ends = [jnp.broadcast_to(rows[r : r + 1, head:], (SLOT, tail)) for r in range(CAP)]
            if head > CAP * tail:
                ends.append(jnp.zeros((SLOT, head - CAP * tail), F32))
            value = jnp.where(down == CAP, jnp.concatenate(ends, axis=1), value)
        out[:, at : at + head] = value.astype(BF16)


def unfolded(pieces, at, width):
    head, tail = folded(width)
    main = jnp.concatenate([p[:, at : at + head] for p in pieces], axis=0)
    if not tail:
        return main
    down = lax.broadcasted_iota(jnp.int32, (SLOT, tail), 0)
    ends = []
    for p in pieces:
        row = p[:, at : at + CAP * tail].astype(F32)[CAP : CAP + 1]
        end = jnp.zeros((SLOT, tail), F32)
        for r in range(CAP):
            end = jnp.where(down == r, row[:, r * tail : (r + 1) * tail], end)
        ends.append(end)
    return jnp.concatenate([main, jnp.concatenate(ends, axis=0).astype(BF16)], axis=1)


def first_spread_body(steps, tokens, *refs):
    small, (state, grad, saved), refs = refs[:4], refs[4:7], refs[7:]
    lines, outs, scratch, sems = refs[0], refs[1 : 1 + EXPERTS], refs[1 + EXPERTS : -1], refs[-1]
    sources = [*small, state, grad, saved.at[pl.ds(0, tokens), :]]
    copies = [
        pltpu.make_async_copy(src, dst, sems.at[i])
        for i, (src, dst) in enumerate(zip(sources, scratch))
    ]
    for copy in copies:
        copy.start()
    lines[...] = jnp.zeros(lines.shape, F32)
    for i in range(4):
        copies[i].wait()
        lines[i * steps : (i + 1) * steps, :tokens] = scratch[i][...].astype(F32)
    routes = jnp.concatenate([scratch[0][0:1], scratch[1][0:1]], axis=0)
    fwd_hits, bwd_hits = slot_hits(routes)
    put_pieces(outs, 0, slot_gates(fwd_hits, bwd_hits, scratch[2][0:1], scratch[3][0:1]))
    fwd_table, bwd_table = as_table(fwd_hits).astype(BF16), as_table(bwd_hits).astype(BF16)
    parts = []
    for i, table in enumerate((fwd_table, bwd_table, bwd_table)):
        copies[4 + i].wait()
        parts.append(placed(table, scratch[4 + i][...]))
    put_folded(outs, LANES, parts)


def first_spread(small, state, grad, saved):
    steps, tokens = small[0].shape
    width = state.shape[1]
    outs = [jax.ShapeDtypeStruct((-(-4 * steps // 8) * 8, LANES), F32)]
    outs += [jax.ShapeDtypeStruct((SLOT, LANES + folded(3 * width)[0]), BF16)] * EXPERTS
    args = [*small, state, grad, saved]
    return call(
        functools.partial(first_spread_body, steps, tokens),
        outs,
        [pltpu.with_memory_space_constraint(a, pltpu.HBM) for a in args],
        in_specs=[pl.BlockSpec(memory_space=pltpu.HBM)] * len(args),
        scratch_shapes=[pltpu.VMEM((steps, tokens), a.dtype) for a in small]
        + [pltpu.VMEM((tokens, width), BF16)] * 3
        + [pltpu.SemaphoreType.DMA((len(args),))],
    )


def prepare_body(steps, tokens, *refs):
    lines, saved, to_tokens, to_slots, gates, later = *refs[:5], refs[5:]
    rank, last = lax.axis_index("pipe"), lax.axis_size("pipe") - 1
    rows = lines[...]
    across = slice(0, tokens)
    for step in range(steps):
        at = (step, steps + step, 2 * steps + step, 3 * steps + step)
        fwd_row, bwd_row, fwd_gate, bwd_gate = (rows[i : i + 1, across] for i in at)
        hits = slot_hits(jnp.concatenate([fwd_row, bwd_row], axis=0))
        gates[step] = slot_gates(*hits, fwd_gate, bwd_gate).astype(BF16)
        for i, end in enumerate((0, last)):
            table = as_table(hits[i])
            to_tokens[2 * step + i] = table.T.astype(BF16)
            come = as_table(hits[i] & (rank != end)).astype(BF16)
            to_slots[2 * step + i] = come
        if step:
            table = table.astype(BF16)
            outs = later[(step - 1) * EXPERTS : step * EXPERTS]
            put_pieces(outs, 0, placed(table, saved[step * tokens : (step + 1) * tokens, :]))


def prepare(lines, saved, steps, tokens):
    slots = EXPERTS * SLOT
    outs = [
        jax.ShapeDtypeStruct((2 * steps, tokens, slots), BF16),
        jax.ShapeDtypeStruct((2 * steps, slots, tokens), BF16),
        jax.ShapeDtypeStruct((steps, slots, LANES), BF16),
    ]
    outs += [jax.ShapeDtypeStruct((SLOT, saved.shape[1]), BF16)] * (EXPERTS * (steps - 1))
    body = functools.partial(prepare_body, steps, tokens)
    to_tokens, to_slots, gates, *later = call(body, outs, [lines, saved])
    later = [later[i * EXPERTS : (i + 1) * EXPERTS] for i in range(steps - 1)]
    return (to_tokens, to_slots, gates), later


def spread_body(step, tables, gates, low, high, *outs):
    even = lax.axis_index("pipe") % 2 == 0
    for m, out in enumerate(outs):
        out[:, :LANES] = gates[step, m * SLOT : (m + 1) * SLOT, :]

    def put(forward, backward):
        parts = [
            placed(tables[2 * step + i], rows[...]) for i, rows in enumerate((forward, backward))
        ]
        put_folded(outs, LANES, parts)

    pl.when(even)(lambda: put(high, low))
    pl.when(jnp.logical_not(even))(lambda: put(low, high))


def gather_body(step, last, tables, *refs):
    pieces, outs = refs[:EXPERTS], refs[EXPERTS:]
    width = outs[0].shape[1]

    slots = unfolded(pieces, 0, 2 * width)

    def put(*targets):
        for stream, out in enumerate(targets):
            rows = slots[:, stream * width : (stream + 1) * width]
            out[...] = placed(tables[2 * step + stream], rows).astype(BF16)

    if last:
        put(*outs)
    else:
        even = lax.axis_index("pipe") % 2 == 0
        pl.when(even)(lambda: put(outs[0], outs[1]))
        pl.when(jnp.logical_not(even))(lambda: put(outs[1], outs[0]))


def weight_targets(outs, j, h):
    _, core = place()
    cols_out, rows_out = outs[:2]
    at = pl.multiple_of((core ^ j) * h, h)
    return (
        cols_out.at[:, pl.ds(at, h)],
        cols_out.at[:, pl.ds(pl.multiple_of(2 * h + at, h), h)],
        rows_out.at[pl.ds(at, h), :],
    )


def flip_weights(outs, j, h):
    _, core = place()
    cols_flip, rows_flip = outs[2:]
    at = pl.multiple_of((core ^ j) * h, h)
    gates, ups, downs = weight_targets(outs, j, h)
    cols_flip[pl.ds(at, h), :] = gates[...].T
    cols_flip[pl.ds(pl.multiple_of(2 * h + at, h), h), :] = ups[...].T
    rows_flip[:, pl.ds(at, h)] = downs[...].T


def pack_own_body(*refs):
    own, outs, sems = refs[:3], refs[3:7], refs[7]
    h = own[0].shape[1]
    copies = [
        pltpu.make_async_copy(src, dst, sems.at[i])
        for i, (src, dst) in enumerate(zip(own, weight_targets(outs, 0, h)))
    ]
    for copy in copies:
        copy.start()
    for copy in copies:
        copy.wait()
    flip_weights(outs, 0, h)


def pack_other_body(*refs):
    other, outs = refs[:3], refs[7:]
    h = other[0].shape[1]
    for src, dst in zip(other, weight_targets(outs, 1, h)):
        dst[...] = src[...]
    flip_weights(outs, 1, h)


def pack(own):
    width, units = own[0].shape
    shapes = ((width, 4 * units), (2 * units, width), (4 * units, width), (width, 2 * units))
    outs = [jax.ShapeDtypeStruct(shape, BF16) for shape in shapes]
    others = [swap_cores(array) for array in own]
    begun = call(
        pack_own_body,
        outs,
        [pltpu.with_memory_space_constraint(array, pltpu.HBM) for array in own],
        in_specs=[pl.BlockSpec(memory_space=pltpu.HBM)] * 3,
        scratch_shapes=[pltpu.SemaphoreType.DMA((3,))],
    )
    return call(
        pack_other_body,
        outs,
        [*others, *begun],
        in_specs=[pl.BlockSpec(memory_space=pltpu.VMEM)] * 7,
        input_output_aliases={3 + i: i for i in range(4)},
    )


def normed_of(rows, gain_ref):
    values = rows.astype(F32)
    mean = jnp.mean(values * values, axis=-1, keepdims=True)
    scale = lax.rsqrt(mean + EPS)
    return scale, (values * scale * gain_ref[...]).astype(BF16)


def expert_body(gain_ref, cols_ref, rows_ref, cols_flip, rows_flip, *refs):
    pieces, outs = refs[:EXPERTS], refs[len(refs) - EXPERTS :]
    n, width = rows_ref.shape
    half = EXPERTS * SLOT

    gates = jnp.concatenate([p[:, :LANES] for p in pieces], axis=0).astype(F32)
    if len(refs) == 2 * EXPERTS:
        slots = unfolded(pieces, LANES, 3 * width)
        saved = slots[:, 2 * width :]
    else:
        slots = unfolded(pieces, LANES, 2 * width)
        saved = jnp.concatenate([p[...] for p in refs[EXPERTS : 2 * EXPERTS]], axis=0)
    state, grad = slots[:, :width], slots[:, width : 2 * width]
    dhidden = jnp.dot(grad, rows_flip[...], preferred_element_type=F32)
    dhidden = dhidden * (gates[:, 2:3] + gates[:, 3:4])
    _, fwd_normed = normed_of(state, gain_ref)
    scale, bwd_normed = normed_of(saved, gain_ref)
    normed = jnp.concatenate([fwd_normed, bwd_normed], axis=0)
    both = jnp.dot(normed, cols_ref[...], preferred_element_type=F32)

    gated, upped = both[:half, :n], both[:half, n:]
    hidden = (gated * jax.nn.sigmoid(gated) * upped).astype(BF16)
    moe = jnp.dot(hidden, rows_ref[...], preferred_element_type=F32)
    new_state = state.astype(F32) + (gates[:, 0:1] + gates[:, 1:2]) * moe

    gated, upped = both[half:, :n], both[half:, n:]
    sigma = jax.nn.sigmoid(gated)
    dgate = (dhidden * upped * sigma * (1.0 + gated * (1.0 - sigma))).astype(BF16)
    dup = (dhidden * gated * sigma).astype(BF16)
    dnorm = jnp.dot(
        jnp.concatenate([dgate, dup], axis=1), cols_flip[...], preferred_element_type=F32
    )
    inner = dgate.astype(F32) * gated + dup.astype(F32) * upped
    mean = jnp.sum(inner, axis=-1, keepdims=True) / width
    value = grad.astype(F32) + scale * (gain_ref[...] * dnorm)
    put_folded(outs, 0, [new_state, value - saved.astype(F32) * (scale * scale * mean)])


def by_home_core(
    fwd_state,
    bwd_state,
    saved_input,
    fwd_route,
    bwd_route,
    fwd_gate,
    bwd_gate,
    w_gate,
    w_up,
    w_down,
    norm_gain,
):
    tokens, width = fwd_state.shape[1:]
    steps = fwd_route.shape[1]
    saved = saved_input[0].reshape(steps * tokens, width)
    small = [a.reshape(steps, tokens) for a in (fwd_route, bwd_route, fwd_gate, bwd_gate)]
    lines, *made = first_spread(small, fwd_state[0], bwd_state[0], saved)
    made, own = lax.optimization_barrier((made, (w_gate[0], w_up[0], w_down[0])))
    pieces = exchange(made)
    weights = pack(own)
    pair = folded(2 * width)[0]
    two = [jax.ShapeDtypeStruct((SLOT, pair), BF16)] * EXPERTS
    main = [jax.ShapeDtypeStruct((SLOT, LANES + pair), BF16)] * EXPERTS
    state = [jax.ShapeDtypeStruct((tokens, width), BF16)] * 2
    tables, later = prepare(lines, saved, steps, tokens)
    weights, tables, later = lax.optimization_barrier((weights, tables, later))
    to_tokens, to_slots, gates = tables
    for step in range(steps):
        back = call(expert_body, two, [norm_gain, *weights, *pieces])
        last = step + 1 == steps
        back = exchange(back)
        body = functools.partial(gather_body, step, last)
        made = call(body, state, [to_tokens, *back])
        if last:
            return made[0][None], made[1][None]
        made, ahead = lax.optimization_barrier((made, later[step]))
        high = swap_ranks(made[1], 1)
        low = swap_ranks(made[0], 0)
        ahead = exchange(ahead)
        body = functools.partial(spread_body, step + 1)
        made = call(body, main, [to_slots, gates, low, high])
        pieces = exchange(made) + ahead


def passed_along(array, axis, by):
    size = lax.axis_size(axis)
    pairs = [(i, i + by) for i in range(size) if 0 <= i + by < size]
    return lax.ppermute(array, axis, pairs)


def norm_rows(rows, gain):
    raw = rows.astype(jnp.float32)
    scale = lax.rsqrt(jnp.mean(raw * raw, axis=-1, keepdims=True) + EPS)
    return (raw, scale, (raw * scale * gain).astype(jnp.bfloat16))


def slot_index(route):
    hits = (route[:, None] == jnp.arange(EXPERTS, dtype=jnp.int32)[None, :]).astype(jnp.int32)
    before = jnp.cumsum(hits, axis=0) - hits
    return route * CAP + jnp.sum(before * hits, axis=1)


def slot_table(index):
    columns = jnp.arange(EXPERTS * CAP, dtype=jnp.int32)
    return (columns[:, None] == index[None, :]).astype(jnp.bfloat16)


def fill_slots(table, rows, shards):
    picked = jnp.dot(table, rows, preferred_element_type=jnp.float32).astype(jnp.bfloat16)
    return jnp.repeat(picked.reshape(EXPERTS, CAP, rows.shape[1]), shards, axis=0)


def collect_rows(returned, index, shards):
    width = returned.shape[2]
    summed = (
        returned.reshape(EXPERTS, shards, returned.shape[1], width).astype(jnp.float32).sum(axis=1)
    )
    return jnp.take(summed.reshape(EXPERTS * CAP, width), index, axis=0)


def by_all_to_all(
    fwd_state,
    bwd_state,
    saved_input,
    fwd_route,
    bwd_route,
    fwd_gate,
    bwd_gate,
    w_gate,
    w_up,
    w_down,
    norm_gain,
):
    shards = lax.axis_size("expert") // EXPERTS
    gain = norm_gain[0]
    gate_cols = w_gate[0]
    up_cols = w_up[0]
    down_rows = w_down[0]
    steps_total = fwd_route.shape[1]
    forward = fwd_state[0]
    backward = bwd_state[0]
    new_forward = forward
    new_backward = backward
    for moment in range(steps_total):
        fwd_index = slot_index(fwd_route[0, moment, :, 0])
        fwd_raw, _, fwd_norm = norm_rows(forward, gain)
        fwd_slots = fill_slots(slot_table(fwd_index), fwd_norm, shards)
        bwd_index = slot_index(bwd_route[0, moment, :, 0])
        bwd_table = slot_table(bwd_index)
        bwd_raw, bwd_scale, bwd_norm = norm_rows(saved_input[0, moment], gain)
        scaled = (bwd_gate[0, moment][:, None] * backward.astype(jnp.float32)).astype(jnp.bfloat16)
        bwd_inputs = fill_slots(bwd_table, bwd_norm, shards)
        bwd_grads = fill_slots(bwd_table, scaled, shards)
        expert_received = lax.all_to_all(
            fwd_slots, "expert", split_axis=0, concat_axis=0, tiled=True
        )
        expert_gated = jnp.einsum(
            "scd,dh->sch", expert_received, gate_cols, preferred_element_type=jnp.float32
        )
        expert_upped = jnp.einsum(
            "scd,dh->sch", expert_received, up_cols, preferred_element_type=jnp.float32
        )
        hidden = (expert_gated * jax.nn.sigmoid(expert_gated) * expert_upped).astype(jnp.bfloat16)
        fwd_partial = jnp.einsum(
            "sch,hd->scd", hidden, down_rows, preferred_element_type=jnp.float32
        ).astype(jnp.bfloat16)
        fwd_back = lax.all_to_all(fwd_partial, "expert", split_axis=0, concat_axis=0, tiled=True)
        inputs_part = lax.all_to_all(bwd_inputs, "expert", split_axis=0, concat_axis=0, tiled=True)
        grads_part = lax.all_to_all(bwd_grads, "expert", split_axis=0, concat_axis=0, tiled=True)
        gated = jnp.einsum(
            "scd,dh->sch", inputs_part, gate_cols, preferred_element_type=jnp.float32
        )
        upped = jnp.einsum("scd,dh->sch", inputs_part, up_cols, preferred_element_type=jnp.float32)
        dhidden = jnp.einsum(
            "scd,hd->sch", grads_part, down_rows, preferred_element_type=jnp.float32
        )
        sigma = jax.nn.sigmoid(gated)
        dgate = (dhidden * upped * sigma * (1.0 + gated * (1.0 - sigma))).astype(jnp.bfloat16)
        dup = (dhidden * gated * sigma).astype(jnp.bfloat16)
        result = jnp.einsum("sch,dh->scd", dgate, gate_cols, preferred_element_type=jnp.float32)
        result = result + jnp.einsum(
            "sch,dh->scd", dup, up_cols, preferred_element_type=jnp.float32
        )
        bwd_partial = result.astype(jnp.bfloat16)
        bwd_back = lax.all_to_all(bwd_partial, "expert", split_axis=0, concat_axis=0, tiled=True)
        moe_rows = collect_rows(fwd_back, fwd_index, shards)
        new_forward = (fwd_raw + fwd_gate[0, moment][:, None] * moe_rows).astype(jnp.bfloat16)
        dnorm = collect_rows(bwd_back, bwd_index, shards)
        weighted = gain * dnorm
        cubed = bwd_scale * bwd_scale * bwd_scale
        dinput = bwd_scale * weighted - bwd_raw * cubed * jnp.mean(
            bwd_raw * weighted, axis=-1, keepdims=True
        )
        new_backward = (backward.astype(jnp.float32) + dinput).astype(jnp.bfloat16)
        if moment + 1 < steps_total:
            forward = passed_along(new_forward, "pipe", 1)
            backward = passed_along(new_backward, "pipe", -1)
    return (new_forward[None], new_backward[None])


def local(*args):
    if lax.axis_size("expert") == 2 * EXPERTS:
        return by_home_core(*args)
    return by_all_to_all(*args)


def solution(mesh):
    specs = (
        P("pipe", "expert", None),
        P("pipe", "expert", None),
        P("pipe", None, "expert", None),
        P("pipe", None, "expert", None),
        P("pipe", None, "expert", None),
        P("pipe", None, "expert"),
        P("pipe", None, "expert"),
        P("pipe", None, "expert"),
        P("pipe", None, "expert"),
        P("pipe", "expert", None),
        P("pipe", None),
    )
    return jax.shard_map(
        local,
        mesh=mesh,
        in_specs=specs,
        out_specs=(P("pipe", "expert", None), P("pipe", "expert", None)),
        check_vma=False,
    )
```

```python
import functools

import jax
import jax.numpy as jnp
from jax import lax
from jax.experimental import pallas as pl
from jax.experimental.pallas import tpu as pltpu
from jax.sharding import PartitionSpec as P

EXPERTS = 4
CAP = 7
EPS = 1e-06


SLOT = -(-CAP // 8) * 8
LANES = 128
F32 = jnp.float32
BF16 = jnp.bfloat16


def call(body, outs, args, vmem=16, **more):
    return pl.pallas_call(
        body,
        out_shape=outs,
        compiler_params=pltpu.CompilerParams(vmem_limit_bytes=vmem * 2**20),
        **more,
    )(*args)


def place():
    device = lax.axis_index("expert")
    return device // 2, device % 2


def swap_cores(array):
    pairs = [(i, i ^ 1) for i in range(lax.axis_size("expert"))]
    return lax.ppermute(array, "expert", pairs)


def exchange(pieces):
    moved = [pieces[0]]
    for m in range(1, EXPERTS):
        pairs = [(i, i ^ (2 * m)) for i in range(lax.axis_size("expert"))]
        moved.append(lax.ppermute(pieces[m], "expert", pairs))
    return moved


def swap_ranks(array, first):
    ranks_total, devices = lax.axis_size("pipe"), lax.axis_size("expert")
    target = [i ^ 1 for i in range(ranks_total * devices)]
    for rank in range(first, ranks_total - 1, 2):
        for i in range(devices):
            a, b = rank * devices + i, (rank + 1) * devices + i
            target[a], target[b] = b, a
    return lax.ppermute(array, ("pipe", "expert"), list(enumerate(target)))


def slot_hits(routes):
    count, tokens = routes.shape
    chip, _ = place()
    routes = routes.astype(jnp.int32)
    expert = lax.broadcasted_iota(jnp.int32, (EXPERTS, tokens), 0)
    named = [jnp.where(expert == routes[i : i + 1], 1.0, 0.0) for i in range(count)]
    down = lax.broadcasted_iota(jnp.int32, (tokens, tokens), 0)
    across = lax.broadcasted_iota(jnp.int32, (tokens, tokens), 1)
    earlier = jnp.where(down < across, 1.0, 0.0).astype(BF16)
    stacked = jnp.concatenate(named, axis=0)
    before = placed(stacked.astype(BF16), earlier) * stacked
    slot = lax.broadcasted_iota(jnp.int32, (EXPERTS * SLOT, tokens), 0)
    hits = []
    for i in range(count):
        rank = jnp.sum(before[i * EXPERTS : (i + 1) * EXPERTS], axis=0, keepdims=True)
        hits.append(slot == (routes[i : i + 1] ^ chip) * SLOT + rank.astype(jnp.int32))
    return hits


def as_table(hits):
    return jnp.where(hits, 1.0, 0.0)


def slot_gates(fwd_hits, bwd_hits, fwd_gates, bwd_gates):
    lane = lax.broadcasted_iota(jnp.int32, (EXPERTS * SLOT, LANES), 1)
    value = jnp.zeros(lane.shape, F32)
    for i, (hits, gates) in enumerate(((fwd_hits, fwd_gates), (bwd_hits, bwd_gates))):
        gate = jnp.sum(jnp.where(hits, gates, 0.0), axis=1, keepdims=True)
        high = gate.astype(BF16).astype(F32)
        value = jnp.where(lane == 2 * i, high, jnp.where(lane == 2 * i + 1, gate - high, value))
    return value


def placed(table, rows):
    return jnp.dot(table, rows, preferred_element_type=F32)


def put_pieces(outs, at, value):
    for m, out in enumerate(outs):
        out[:, at : at + value.shape[1]] = value[m * SLOT : (m + 1) * SLOT].astype(BF16)


def folded(width):
    if SLOT == CAP:
        return width, 0
    tail = width // LANES // (CAP + 1) * LANES
    return width - tail, tail


def put_folded(outs, at, parts):
    head, tail = folded(sum(p.shape[1] for p in parts))
    down = lax.broadcasted_iota(jnp.int32, (SLOT, head), 0)
    for m, out in enumerate(outs):
        rows = jnp.concatenate([p[m * SLOT : (m + 1) * SLOT] for p in parts], axis=1)
        value = rows[:, :head]
        if tail:
            ends = [jnp.broadcast_to(rows[r : r + 1, head:], (SLOT, tail)) for r in range(CAP)]
            if head > CAP * tail:
                ends.append(jnp.zeros((SLOT, head - CAP * tail), F32))
            value = jnp.where(down == CAP, jnp.concatenate(ends, axis=1), value)
        out[:, at : at + head] = value.astype(BF16)


def unfolded(pieces, at, width):
    head, tail = folded(width)
    main = jnp.concatenate([p[:, at : at + head] for p in pieces], axis=0)
    if not tail:
        return main
    down = lax.broadcasted_iota(jnp.int32, (SLOT, tail), 0)
    ends = []
    for p in pieces:
        row = p[:, at : at + CAP * tail].astype(F32)[CAP : CAP + 1]
        end = jnp.zeros((SLOT, tail), F32)
        for r in range(CAP):
            end = jnp.where(down == r, row[:, r * tail : (r + 1) * tail], end)
        ends.append(end)
    return jnp.concatenate([main, jnp.concatenate(ends, axis=0).astype(BF16)], axis=1)


def first_spread_body(steps, tokens, *refs):
    small, (state, grad, saved), refs = refs[:4], refs[4:7], refs[7:]
    lines, held, tables, gates, out, scratch, sems = (
        refs[0], refs[1:4], refs[4], refs[5], refs[6], refs[7:-1], refs[-1]
    )
    sources = [*small, state, grad, saved.at[pl.ds(0, tokens), :]]
    copies = [
        pltpu.make_async_copy(src, dst, sems.at[i])
        for i, (src, dst) in enumerate(zip(sources, [*scratch, *held]))
    ]
    for copy in copies:
        copy.start()
    lines[...] = jnp.zeros(lines.shape, F32)
    for i in range(4):
        copies[i].wait()
        lines[i * steps : (i + 1) * steps, :tokens] = scratch[i][...].astype(F32)
    routes = jnp.concatenate([scratch[0][0:1], scratch[1][0:1]], axis=0)
    hits = slot_hits(routes)
    value = slot_gates(*hits, scratch[2][0:1], scratch[3][0:1])
    gates[...] = value.astype(BF16)
    near = (EXPERTS - 1) * SLOT
    put_pieces([out], 0, value[near:])
    made = [as_table(h) for h in hits]
    for i, table in enumerate(made):
        tables[i] = table.astype(BF16)
    far = [table[near:].astype(BF16) for table in made]
    parts = []
    for i, table in enumerate((far[0], far[1], far[1])):
        copies[4 + i].wait()
        parts.append(placed(table, held[i][...]))
    put_folded([out], LANES, parts)


def other_spread_body(tables, gates, state, grad, saved, *outs):
    near = (EXPERTS - 1) * SLOT
    put_pieces(outs, 0, gates[:near, :].astype(F32))
    pairs = ((tables[0], state), (tables[1], grad), (tables[1], saved))
    put_folded(outs, LANES, [placed(table[:near], rows[...]) for table, rows in pairs])


def first_spread(small, state, grad, saved):
    steps, tokens = small[0].shape
    width = state.shape[1]
    slots = EXPERTS * SLOT
    piece = jax.ShapeDtypeStruct((SLOT, LANES + folded(3 * width)[0]), BF16)
    outs = [jax.ShapeDtypeStruct((-(-4 * steps // 8) * 8, LANES), F32)]
    outs += [jax.ShapeDtypeStruct((tokens, width), BF16)] * 3
    outs += [jax.ShapeDtypeStruct((2, slots, tokens), BF16)]
    outs += [jax.ShapeDtypeStruct((slots, LANES), BF16), piece]
    args = [*small, state, grad, saved]
    lines, *held, tables, gates, far = call(
        functools.partial(first_spread_body, steps, tokens),
        outs,
        [pltpu.with_memory_space_constraint(a, pltpu.HBM) for a in args],
        in_specs=[pl.BlockSpec(memory_space=pltpu.HBM)] * len(args),
        scratch_shapes=[pltpu.VMEM((steps, tokens), a.dtype) for a in small]
        + [pltpu.SemaphoreType.DMA((len(args),))],
    )
    near = call(other_spread_body, [piece] * (EXPERTS - 1), [tables, gates, *held])
    return lines, *near, far


def prepare_body(steps, tokens, *refs):
    lines, saved, to_tokens, to_slots, gates, later = *refs[:5], refs[5:]
    rank, last = lax.axis_index("pipe"), lax.axis_size("pipe") - 1
    rows = lines[...]
    across = slice(0, tokens)
    for step in range(steps):
        at = (step, steps + step, 2 * steps + step, 3 * steps + step)
        fwd_row, bwd_row, fwd_gate, bwd_gate = (rows[i : i + 1, across] for i in at)
        hits = slot_hits(jnp.concatenate([fwd_row, bwd_row], axis=0))
        gates[step] = slot_gates(*hits, fwd_gate, bwd_gate).astype(BF16)
        for i, end in enumerate((0, last)):
            table = as_table(hits[i])
            to_tokens[2 * step + i] = table.T.astype(BF16)
            come = as_table(hits[i] & (rank != end)).astype(BF16)
            to_slots[2 * step + i] = come
        if step:
            table = table.astype(BF16)
            outs = later[(step - 1) * EXPERTS : step * EXPERTS]
            put_pieces(outs, 0, placed(table, saved[step * tokens : (step + 1) * tokens, :]))


def prepare(lines, saved, steps, tokens):
    slots = EXPERTS * SLOT
    outs = [
        jax.ShapeDtypeStruct((2 * steps, tokens, slots), BF16),
        jax.ShapeDtypeStruct((2 * steps, slots, tokens), BF16),
        jax.ShapeDtypeStruct((steps, slots, LANES), BF16),
    ]
    outs += [jax.ShapeDtypeStruct((SLOT, saved.shape[1]), BF16)] * (EXPERTS * (steps - 1))
    body = functools.partial(prepare_body, steps, tokens)
    to_tokens, to_slots, gates, *later = call(body, outs, [lines, saved])
    later = [later[i * EXPERTS : (i + 1) * EXPERTS] for i in range(steps - 1)]
    return (to_tokens, to_slots, gates), later


def spread_body(step, tables, gates, low, high, *outs):
    even = lax.axis_index("pipe") % 2 == 0
    for m, out in enumerate(outs):
        out[:, :LANES] = gates[step, m * SLOT : (m + 1) * SLOT, :]

    def put(forward, backward):
        parts = [
            placed(tables[2 * step + i], rows[...]) for i, rows in enumerate((forward, backward))
        ]
        put_folded(outs, LANES, parts)

    pl.when(even)(lambda: put(high, low))
    pl.when(jnp.logical_not(even))(lambda: put(low, high))


def gather_body(step, last, tables, *refs):
    pieces, outs = refs[:EXPERTS], refs[EXPERTS:]
    width = outs[0].shape[1]

    slots = unfolded(pieces, 0, 2 * width)

    def put(*targets):
        for stream, out in enumerate(targets):
            rows = slots[:, stream * width : (stream + 1) * width]
            out[...] = placed(tables[2 * step + stream], rows).astype(BF16)

    if last:
        put(*outs)
    else:
        even = lax.axis_index("pipe") % 2 == 0
        pl.when(even)(lambda: put(outs[0], outs[1]))
        pl.when(jnp.logical_not(even))(lambda: put(outs[1], outs[0]))


def weight_targets(outs, j, h):
    _, core = place()
    cols_out, rows_out = outs[:2]
    at = pl.multiple_of((core ^ j) * h, h)
    return (
        cols_out.at[:, pl.ds(at, h)],
        cols_out.at[:, pl.ds(pl.multiple_of(2 * h + at, h), h)],
        rows_out.at[pl.ds(at, h), :],
    )


def flip_weights(outs, j, h):
    _, core = place()
    cols_flip, rows_flip = outs[2:]
    at = pl.multiple_of((core ^ j) * h, h)
    gates, ups, downs = weight_targets(outs, j, h)
    cols_flip[pl.ds(at, h), :] = gates[...].T
    cols_flip[pl.ds(pl.multiple_of(2 * h + at, h), h), :] = ups[...].T
    rows_flip[:, pl.ds(at, h)] = downs[...].T


def pack_own_body(*refs):
    own, outs, sems = refs[:3], refs[3:7], refs[7]
    h = own[0].shape[1]
    copies = [
        pltpu.make_async_copy(src, dst, sems.at[i])
        for i, (src, dst) in enumerate(zip(own, weight_targets(outs, 0, h)))
    ]
    for copy in copies:
        copy.start()
    for copy in copies:
        copy.wait()
    flip_weights(outs, 0, h)


def pack_other_body(*refs):
    other, outs = refs[:3], refs[7:]
    h = other[0].shape[1]
    for src, dst in zip(other, weight_targets(outs, 1, h)):
        dst[...] = src[...]
    flip_weights(outs, 1, h)


def pack(own):
    width, units = own[0].shape
    shapes = ((width, 4 * units), (2 * units, width), (4 * units, width), (width, 2 * units))
    outs = [jax.ShapeDtypeStruct(shape, BF16) for shape in shapes]
    others = [swap_cores(array) for array in own]
    begun = call(
        pack_own_body,
        outs,
        [pltpu.with_memory_space_constraint(array, pltpu.HBM) for array in own],
        in_specs=[pl.BlockSpec(memory_space=pltpu.HBM)] * 3,
        scratch_shapes=[pltpu.SemaphoreType.DMA((3,))],
    )
    return call(
        pack_other_body,
        outs,
        [*others, *begun],
        in_specs=[pl.BlockSpec(memory_space=pltpu.VMEM)] * 7,
        input_output_aliases={3 + i: i for i in range(4)},
    )


def normed_of(rows, gain_ref):
    values = rows.astype(F32)
    mean = jnp.mean(values * values, axis=-1, keepdims=True)
    scale = lax.rsqrt(mean + EPS)
    return scale, (values * scale * gain_ref[...]).astype(BF16)


def expert_body(gain_ref, cols_ref, rows_ref, cols_flip, rows_flip, *refs):
    pieces, outs = refs[:EXPERTS], refs[len(refs) - EXPERTS :]
    n, width = rows_ref.shape
    half = EXPERTS * SLOT

    gates = jnp.concatenate([p[:, :LANES] for p in pieces], axis=0).astype(F32)
    if len(refs) == 2 * EXPERTS:
        slots = unfolded(pieces, LANES, 3 * width)
        saved = slots[:, 2 * width :]
    else:
        slots = unfolded(pieces, LANES, 2 * width)
        saved = jnp.concatenate([p[...] for p in refs[EXPERTS : 2 * EXPERTS]], axis=0)
    state, grad = slots[:, :width], slots[:, width : 2 * width]
    dhidden = jnp.dot(grad, rows_flip[...], preferred_element_type=F32)
    dhidden = dhidden * (gates[:, 2:3] + gates[:, 3:4])
    _, fwd_normed = normed_of(state, gain_ref)
    scale, bwd_normed = normed_of(saved, gain_ref)
    normed = jnp.concatenate([fwd_normed, bwd_normed], axis=0)
    both = jnp.dot(normed, cols_ref[...], preferred_element_type=F32)

    gated, upped = both[:half, :n], both[:half, n:]
    hidden = (gated * jax.nn.sigmoid(gated) * upped).astype(BF16)
    moe = jnp.dot(hidden, rows_ref[...], preferred_element_type=F32)
    new_state = state.astype(F32) + (gates[:, 0:1] + gates[:, 1:2]) * moe

    gated, upped = both[half:, :n], both[half:, n:]
    sigma = jax.nn.sigmoid(gated)
    dgate = (dhidden * upped * sigma * (1.0 + gated * (1.0 - sigma))).astype(BF16)
    dup = (dhidden * gated * sigma).astype(BF16)
    dnorm = jnp.dot(
        jnp.concatenate([dgate, dup], axis=1), cols_flip[...], preferred_element_type=F32
    )
    inner = dgate.astype(F32) * gated + dup.astype(F32) * upped
    mean = jnp.sum(inner, axis=-1, keepdims=True) / width
    value = grad.astype(F32) + scale * (gain_ref[...] * dnorm)
    put_folded(outs, 0, [new_state, value - saved.astype(F32) * (scale * scale * mean)])


def by_home_core(
    fwd_state,
    bwd_state,
    saved_input,
    fwd_route,
    bwd_route,
    fwd_gate,
    bwd_gate,
    w_gate,
    w_up,
    w_down,
    norm_gain,
):
    tokens, width = fwd_state.shape[1:]
    steps = fwd_route.shape[1]
    saved = saved_input[0].reshape(steps * tokens, width)
    small = [a.reshape(steps, tokens) for a in (fwd_route, bwd_route, fwd_gate, bwd_gate)]
    lines, *made = first_spread(small, fwd_state[0], bwd_state[0], saved)
    lines, own = lax.optimization_barrier((lines, (w_gate[0], w_up[0], w_down[0])))
    pieces = exchange(made)
    weights = pack(own)
    pair = folded(2 * width)[0]
    two = [jax.ShapeDtypeStruct((SLOT, pair), BF16)] * EXPERTS
    main = [jax.ShapeDtypeStruct((SLOT, LANES + pair), BF16)] * EXPERTS
    state = [jax.ShapeDtypeStruct((tokens, width), BF16)] * 2
    tables, later = prepare(lines, saved, steps, tokens)
    weights, tables, later = lax.optimization_barrier((weights, tables, later))
    to_tokens, to_slots, gates = tables
    for step in range(steps):
        back = call(expert_body, two, [norm_gain, *weights, *pieces])
        last = step + 1 == steps
        back = exchange(back)
        body = functools.partial(gather_body, step, last)
        made = call(body, state, [to_tokens, *back])
        if last:
            return made[0][None], made[1][None]
        made, ahead = lax.optimization_barrier((made, later[step]))
        high = swap_ranks(made[1], 1)
        low = swap_ranks(made[0], 0)
        ahead = exchange(ahead)
        body = functools.partial(spread_body, step + 1)
        made = call(body, main, [to_slots, gates, low, high])
        pieces = exchange(made) + ahead


def passed_along(array, axis, by):
    size = lax.axis_size(axis)
    pairs = [(i, i + by) for i in range(size) if 0 <= i + by < size]
    return lax.ppermute(array, axis, pairs)


def norm_rows(rows, gain):
    raw = rows.astype(jnp.float32)
    scale = lax.rsqrt(jnp.mean(raw * raw, axis=-1, keepdims=True) + EPS)
    return (raw, scale, (raw * scale * gain).astype(jnp.bfloat16))


def slot_index(route):
    hits = (route[:, None] == jnp.arange(EXPERTS, dtype=jnp.int32)[None, :]).astype(jnp.int32)
    before = jnp.cumsum(hits, axis=0) - hits
    return route * CAP + jnp.sum(before * hits, axis=1)


def slot_table(index):
    columns = jnp.arange(EXPERTS * CAP, dtype=jnp.int32)
    return (columns[:, None] == index[None, :]).astype(jnp.bfloat16)


def fill_slots(table, rows, shards):
    picked = jnp.dot(table, rows, preferred_element_type=jnp.float32).astype(jnp.bfloat16)
    return jnp.repeat(picked.reshape(EXPERTS, CAP, rows.shape[1]), shards, axis=0)


def collect_rows(returned, index, shards):
    width = returned.shape[2]
    summed = (
        returned.reshape(EXPERTS, shards, returned.shape[1], width).astype(jnp.float32).sum(axis=1)
    )
    return jnp.take(summed.reshape(EXPERTS * CAP, width), index, axis=0)


def by_all_to_all(
    fwd_state,
    bwd_state,
    saved_input,
    fwd_route,
    bwd_route,
    fwd_gate,
    bwd_gate,
    w_gate,
    w_up,
    w_down,
    norm_gain,
):
    shards = lax.axis_size("expert") // EXPERTS
    gain = norm_gain[0]
    gate_cols = w_gate[0]
    up_cols = w_up[0]
    down_rows = w_down[0]
    steps_total = fwd_route.shape[1]
    forward = fwd_state[0]
    backward = bwd_state[0]
    new_forward = forward
    new_backward = backward
    for moment in range(steps_total):
        fwd_index = slot_index(fwd_route[0, moment, :, 0])
        fwd_raw, _, fwd_norm = norm_rows(forward, gain)
        fwd_slots = fill_slots(slot_table(fwd_index), fwd_norm, shards)
        bwd_index = slot_index(bwd_route[0, moment, :, 0])
        bwd_table = slot_table(bwd_index)
        bwd_raw, bwd_scale, bwd_norm = norm_rows(saved_input[0, moment], gain)
        scaled = (bwd_gate[0, moment][:, None] * backward.astype(jnp.float32)).astype(jnp.bfloat16)
        bwd_inputs = fill_slots(bwd_table, bwd_norm, shards)
        bwd_grads = fill_slots(bwd_table, scaled, shards)
        expert_received = lax.all_to_all(
            fwd_slots, "expert", split_axis=0, concat_axis=0, tiled=True
        )
        expert_gated = jnp.einsum(
            "scd,dh->sch", expert_received, gate_cols, preferred_element_type=jnp.float32
        )
        expert_upped = jnp.einsum(
            "scd,dh->sch", expert_received, up_cols, preferred_element_type=jnp.float32
        )
        hidden = (expert_gated * jax.nn.sigmoid(expert_gated) * expert_upped).astype(jnp.bfloat16)
        fwd_partial = jnp.einsum(
            "sch,hd->scd", hidden, down_rows, preferred_element_type=jnp.float32
        ).astype(jnp.bfloat16)
        fwd_back = lax.all_to_all(fwd_partial, "expert", split_axis=0, concat_axis=0, tiled=True)
        inputs_part = lax.all_to_all(bwd_inputs, "expert", split_axis=0, concat_axis=0, tiled=True)
        grads_part = lax.all_to_all(bwd_grads, "expert", split_axis=0, concat_axis=0, tiled=True)
        gated = jnp.einsum(
            "scd,dh->sch", inputs_part, gate_cols, preferred_element_type=jnp.float32
        )
        upped = jnp.einsum("scd,dh->sch", inputs_part, up_cols, preferred_element_type=jnp.float32)
        dhidden = jnp.einsum(
            "scd,hd->sch", grads_part, down_rows, preferred_element_type=jnp.float32
        )
        sigma = jax.nn.sigmoid(gated)
        dgate = (dhidden * upped * sigma * (1.0 + gated * (1.0 - sigma))).astype(jnp.bfloat16)
        dup = (dhidden * gated * sigma).astype(jnp.bfloat16)
        result = jnp.einsum("sch,dh->scd", dgate, gate_cols, preferred_element_type=jnp.float32)
        result = result + jnp.einsum(
            "sch,dh->scd", dup, up_cols, preferred_element_type=jnp.float32
        )
        bwd_partial = result.astype(jnp.bfloat16)
        bwd_back = lax.all_to_all(bwd_partial, "expert", split_axis=0, concat_axis=0, tiled=True)
        moe_rows = collect_rows(fwd_back, fwd_index, shards)
        new_forward = (fwd_raw + fwd_gate[0, moment][:, None] * moe_rows).astype(jnp.bfloat16)
        dnorm = collect_rows(bwd_back, bwd_index, shards)
        weighted = gain * dnorm
        cubed = bwd_scale * bwd_scale * bwd_scale
        dinput = bwd_scale * weighted - bwd_raw * cubed * jnp.mean(
            bwd_raw * weighted, axis=-1, keepdims=True
        )
        new_backward = (backward.astype(jnp.float32) + dinput).astype(jnp.bfloat16)
        if moment + 1 < steps_total:
            forward = passed_along(new_forward, "pipe", 1)
            backward = passed_along(new_backward, "pipe", -1)
    return (new_forward[None], new_backward[None])


def local(*args):
    if lax.axis_size("expert") == 2 * EXPERTS:
        return by_home_core(*args)
    return by_all_to_all(*args)


def solution(mesh):
    specs = (
        P("pipe", "expert", None),
        P("pipe", "expert", None),
        P("pipe", None, "expert", None),
        P("pipe", None, "expert", None),
        P("pipe", None, "expert", None),
        P("pipe", None, "expert"),
        P("pipe", None, "expert"),
        P("pipe", None, "expert"),
        P("pipe", None, "expert"),
        P("pipe", "expert", None),
        P("pipe", None),
    )
    return jax.shard_map(
        local,
        mesh=mesh,
        in_specs=specs,
        out_specs=(P("pipe", "expert", None), P("pipe", "expert", None)),
        check_vma=False,
    )
```

```python
import functools

import jax
import jax.numpy as jnp
from jax import lax
from jax.experimental import pallas as pl
from jax.experimental.pallas import tpu as pltpu
from jax.sharding import PartitionSpec as P

EXPERTS = 4
CAP = 7
EPS = 1e-06


SLOT = -(-CAP // 8) * 8
LANES = 128
F32 = jnp.float32
BF16 = jnp.bfloat16


def call(body, outs, args, vmem=16, **more):
    return pl.pallas_call(
        body,
        out_shape=outs,
        compiler_params=pltpu.CompilerParams(vmem_limit_bytes=vmem * 2**20),
        **more,
    )(*args)


def place():
    device = lax.axis_index("expert")
    return device // 2, device % 2


def swap_cores(array):
    pairs = [(i, i ^ 1) for i in range(lax.axis_size("expert"))]
    return lax.ppermute(array, "expert", pairs)


def exchange(pieces):
    moved = [pieces[0]]
    for m in range(1, EXPERTS):
        pairs = [(i, i ^ (2 * m)) for i in range(lax.axis_size("expert"))]
        moved.append(lax.ppermute(pieces[m], "expert", pairs))
    return moved


def swap_ranks(array, first):
    ranks_total, devices = lax.axis_size("pipe"), lax.axis_size("expert")
    target = [i ^ 1 for i in range(ranks_total * devices)]
    for rank in range(first, ranks_total - 1, 2):
        for i in range(devices):
            a, b = rank * devices + i, (rank + 1) * devices + i
            target[a], target[b] = b, a
    return lax.ppermute(array, ("pipe", "expert"), list(enumerate(target)))


def slot_hits(routes):
    count, tokens = routes.shape
    chip, _ = place()
    routes = routes.astype(jnp.int32)
    expert = lax.broadcasted_iota(jnp.int32, (EXPERTS, tokens), 0)
    named = [jnp.where(expert == routes[i : i + 1], 1.0, 0.0) for i in range(count)]
    down = lax.broadcasted_iota(jnp.int32, (tokens, tokens), 0)
    across = lax.broadcasted_iota(jnp.int32, (tokens, tokens), 1)
    earlier = jnp.where(down < across, 1.0, 0.0).astype(BF16)
    stacked = jnp.concatenate(named, axis=0)
    before = placed(stacked.astype(BF16), earlier) * stacked
    slot = lax.broadcasted_iota(jnp.int32, (EXPERTS * SLOT, tokens), 0)
    hits = []
    for i in range(count):
        rank = jnp.sum(before[i * EXPERTS : (i + 1) * EXPERTS], axis=0, keepdims=True)
        hits.append(slot == (routes[i : i + 1] ^ chip) * SLOT + rank.astype(jnp.int32))
    return hits


def as_table(hits):
    return jnp.where(hits, 1.0, 0.0)


def slot_gates(fwd_hits, bwd_hits, fwd_gates, bwd_gates):
    lane = lax.broadcasted_iota(jnp.int32, (EXPERTS * SLOT, LANES), 1)
    value = jnp.zeros(lane.shape, F32)
    for i, (hits, gates) in enumerate(((fwd_hits, fwd_gates), (bwd_hits, bwd_gates))):
        gate = jnp.sum(jnp.where(hits, gates, 0.0), axis=1, keepdims=True)
        high = gate.astype(BF16).astype(F32)
        value = jnp.where(lane == 2 * i, high, jnp.where(lane == 2 * i + 1, gate - high, value))
    return value


def placed(table, rows):
    return jnp.dot(table, rows, preferred_element_type=F32)


def put_pieces(outs, at, value):
    for m, out in enumerate(outs):
        out[:, at : at + value.shape[1]] = value[m * SLOT : (m + 1) * SLOT].astype(BF16)


def folded(width):
    if SLOT == CAP:
        return width, 0
    tail = width // LANES // (CAP + 1) * LANES
    return width - tail, tail


def put_folded(outs, at, parts):
    head, tail = folded(sum(p.shape[1] for p in parts))
    down = lax.broadcasted_iota(jnp.int32, (SLOT, head), 0)
    for m, out in enumerate(outs):
        rows = jnp.concatenate([p[m * SLOT : (m + 1) * SLOT] for p in parts], axis=1)
        value = rows[:, :head]
        if tail:
            ends = [jnp.broadcast_to(rows[r : r + 1, head:], (SLOT, tail)) for r in range(CAP)]
            if head > CAP * tail:
                ends.append(jnp.zeros((SLOT, head - CAP * tail), F32))
            value = jnp.where(down == CAP, jnp.concatenate(ends, axis=1), value)
        out[:, at : at + head] = value.astype(BF16)


def unfolded(pieces, at, width):
    head, tail = folded(width)
    main = jnp.concatenate([p[:, at : at + head] for p in pieces], axis=0)
    if not tail:
        return main
    down = lax.broadcasted_iota(jnp.int32, (SLOT, tail), 0)
    ends = []
    for p in pieces:
        row = p[:, at : at + CAP * tail].astype(F32)[CAP : CAP + 1]
        end = jnp.zeros((SLOT, tail), F32)
        for r in range(CAP):
            end = jnp.where(down == r, row[:, r * tail : (r + 1) * tail], end)
        ends.append(end)
    return jnp.concatenate([main, jnp.concatenate(ends, axis=0).astype(BF16)], axis=1)


def first_spread_body(steps, tokens, *refs):
    small, (state, grad, saved), refs = refs[:4], refs[4:7], refs[7:]
    lines, held, tables, gates, out, scratch, sems = (
        refs[0], refs[1:4], refs[4], refs[5], refs[6], refs[7:-1], refs[-1]
    )
    sources = [*small, state, grad, saved.at[pl.ds(0, tokens), :]]
    copies = [
        pltpu.make_async_copy(src, dst, sems.at[i])
        for i, (src, dst) in enumerate(zip(sources, [*scratch, *held]))
    ]
    for copy in copies:
        copy.start()
    lines[...] = jnp.zeros(lines.shape, F32)
    for i in range(4):
        copies[i].wait()
        lines[i * steps : (i + 1) * steps, :tokens] = scratch[i][...].astype(F32)
    routes = jnp.concatenate([scratch[0][0:1], scratch[1][0:1]], axis=0)
    hits = slot_hits(routes)
    value = slot_gates(*hits, scratch[2][0:1], scratch[3][0:1])
    gates[...] = value.astype(BF16)
    near = (EXPERTS - 1) * SLOT
    put_pieces([out], 0, value[near:])
    made = [as_table(h) for h in hits]
    for i, table in enumerate(made):
        tables[i] = table.astype(BF16)
    far = [table[near:].astype(BF16) for table in made]
    parts = []
    for i, table in enumerate((far[0], far[1], far[1])):
        copies[4 + i].wait()
        parts.append(placed(table, held[i][...]))
    put_folded([out], LANES, parts)


def other_spread_body(tables, gates, state, grad, saved, *outs):
    near = (EXPERTS - 1) * SLOT
    put_pieces(outs, 0, gates[:near, :].astype(F32))
    pairs = ((tables[0], state), (tables[1], grad), (tables[1], saved))
    put_folded(outs, LANES, [placed(table[:near], rows[...]) for table, rows in pairs])


def first_spread(small, state, grad, saved):
    steps, tokens = small[0].shape
    width = state.shape[1]
    slots = EXPERTS * SLOT
    piece = jax.ShapeDtypeStruct((SLOT, LANES + folded(3 * width)[0]), BF16)
    outs = [jax.ShapeDtypeStruct((-(-4 * steps // 8) * 8, LANES), F32)]
    outs += [jax.ShapeDtypeStruct((tokens, width), BF16)] * 3
    outs += [jax.ShapeDtypeStruct((2, slots, tokens), BF16)]
    outs += [jax.ShapeDtypeStruct((slots, LANES), BF16), piece]
    args = [*small, state, grad, saved]
    lines, *held, tables, gates, far = call(
        functools.partial(first_spread_body, steps, tokens),
        outs,
        [pltpu.with_memory_space_constraint(a, pltpu.HBM) for a in args],
        in_specs=[pl.BlockSpec(memory_space=pltpu.HBM)] * len(args),
        scratch_shapes=[pltpu.VMEM((steps, tokens), a.dtype) for a in small]
        + [pltpu.SemaphoreType.DMA((len(args),))],
    )
    near = call(other_spread_body, [piece] * (EXPERTS - 1), [tables, gates, *held])
    return lines, *near, far


def prepare_body(steps, tokens, *refs):
    lines, saved, to_tokens, to_slots, gates, later = *refs[:5], refs[5:]
    rank, last = lax.axis_index("pipe"), lax.axis_size("pipe") - 1
    rows = lines[...]
    across = slice(0, tokens)
    for step in range(steps):
        at = (step, steps + step, 2 * steps + step, 3 * steps + step)
        fwd_row, bwd_row, fwd_gate, bwd_gate = (rows[i : i + 1, across] for i in at)
        hits = slot_hits(jnp.concatenate([fwd_row, bwd_row], axis=0))
        gates[step] = slot_gates(*hits, fwd_gate, bwd_gate).astype(BF16)
        for i, end in enumerate((0, last)):
            table = as_table(hits[i])
            to_tokens[2 * step + i] = table.T.astype(BF16)
            come = as_table(hits[i] & (rank != end)).astype(BF16)
            to_slots[2 * step + i] = come
        if step:
            table = table.astype(BF16)
            outs = later[(step - 1) * EXPERTS : step * EXPERTS]
            put_pieces(outs, 0, placed(table, saved[step * tokens : (step + 1) * tokens, :]))


def prepare(lines, saved, steps, tokens):
    slots = EXPERTS * SLOT
    outs = [
        jax.ShapeDtypeStruct((2 * steps, tokens, slots), BF16),
        jax.ShapeDtypeStruct((2 * steps, slots, tokens), BF16),
        jax.ShapeDtypeStruct((steps, slots, LANES), BF16),
    ]
    outs += [jax.ShapeDtypeStruct((SLOT, saved.shape[1]), BF16)] * (EXPERTS * (steps - 1))
    body = functools.partial(prepare_body, steps, tokens)
    to_tokens, to_slots, gates, *later = call(body, outs, [lines, saved])
    later = [later[i * EXPERTS : (i + 1) * EXPERTS] for i in range(steps - 1)]
    return (to_tokens, to_slots, gates), later


def spread_body(step, begin, tables, gates, low, high, *outs):
    even = lax.axis_index("pipe") % 2 == 0
    span = slice(begin * SLOT, (begin + len(outs)) * SLOT)
    for m, out in enumerate(outs):
        out[:, :LANES] = gates[step, (begin + m) * SLOT : (begin + m + 1) * SLOT, :]

    def put(forward, backward):
        parts = [
            placed(tables[2 * step + i][span], rows[...])
            for i, rows in enumerate((forward, backward))
        ]
        put_folded(outs, LANES, parts)

    pl.when(even)(lambda: put(high, low))
    pl.when(jnp.logical_not(even))(lambda: put(low, high))


def gather_body(step, last, tables, *refs):
    pieces, outs = refs[:EXPERTS], refs[EXPERTS:]
    width = outs[0].shape[1]

    slots = unfolded(pieces, 0, 2 * width)

    def put(*targets):
        for stream, out in enumerate(targets):
            rows = slots[:, stream * width : (stream + 1) * width]
            out[...] = placed(tables[2 * step + stream], rows).astype(BF16)

    if last:
        put(*outs)
    else:
        even = lax.axis_index("pipe") % 2 == 0
        pl.when(even)(lambda: put(outs[0], outs[1]))
        pl.when(jnp.logical_not(even))(lambda: put(outs[1], outs[0]))


def weight_targets(outs, j, h):
    _, core = place()
    cols_out, rows_out = outs[:2]
    at = pl.multiple_of((core ^ j) * h, h)
    return (
        cols_out.at[:, pl.ds(at, h)],
        cols_out.at[:, pl.ds(pl.multiple_of(2 * h + at, h), h)],
        rows_out.at[pl.ds(at, h), :],
    )


def flip_weights(outs, j, h):
    _, core = place()
    cols_flip, rows_flip = outs[2:]
    at = pl.multiple_of((core ^ j) * h, h)
    gates, ups, downs = weight_targets(outs, j, h)
    cols_flip[pl.ds(at, h), :] = gates[...].T
    cols_flip[pl.ds(pl.multiple_of(2 * h + at, h), h), :] = ups[...].T
    rows_flip[:, pl.ds(at, h)] = downs[...].T


def pack_own_body(*refs):
    own, outs, sems = refs[:3], refs[3:7], refs[7]
    h = own[0].shape[1]
    copies = [
        pltpu.make_async_copy(src, dst, sems.at[i])
        for i, (src, dst) in enumerate(zip(own, weight_targets(outs, 0, h)))
    ]
    for copy in copies:
        copy.start()
    for copy in copies:
        copy.wait()
    flip_weights(outs, 0, h)


def pack_other_body(*refs):
    other, outs = refs[:3], refs[7:]
    h = other[0].shape[1]
    for src, dst in zip(other, weight_targets(outs, 1, h)):
        dst[...] = src[...]
    flip_weights(outs, 1, h)


def pack(own):
    width, units = own[0].shape
    shapes = ((width, 4 * units), (2 * units, width), (4 * units, width), (width, 2 * units))
    outs = [jax.ShapeDtypeStruct(shape, BF16) for shape in shapes]
    others = [swap_cores(array) for array in own]
    begun = call(
        pack_own_body,
        outs,
        [pltpu.with_memory_space_constraint(array, pltpu.HBM) for array in own],
        in_specs=[pl.BlockSpec(memory_space=pltpu.HBM)] * 3,
        scratch_shapes=[pltpu.SemaphoreType.DMA((3,))],
    )
    return call(
        pack_other_body,
        outs,
        [*others, *begun],
        in_specs=[pl.BlockSpec(memory_space=pltpu.VMEM)] * 7,
        input_output_aliases={3 + i: i for i in range(4)},
    )


def normed_of(rows, gain_ref):
    values = rows.astype(F32)
    mean = jnp.mean(values * values, axis=-1, keepdims=True)
    scale = lax.rsqrt(mean + EPS)
    return scale, (values * scale * gain_ref[...]).astype(BF16)


def expert_body(gain_ref, cols_ref, rows_ref, cols_flip, rows_flip, *refs):
    pieces, outs = refs[:EXPERTS], refs[len(refs) - EXPERTS :]
    n, width = rows_ref.shape
    half = EXPERTS * SLOT

    gates = jnp.concatenate([p[:, :LANES] for p in pieces], axis=0).astype(F32)
    if len(refs) == 2 * EXPERTS:
        slots = unfolded(pieces, LANES, 3 * width)
        saved = slots[:, 2 * width :]
    else:
        slots = unfolded(pieces, LANES, 2 * width)
        saved = jnp.concatenate([p[...] for p in refs[EXPERTS : 2 * EXPERTS]], axis=0)
    state, grad = slots[:, :width], slots[:, width : 2 * width]
    dhidden = jnp.dot(grad, rows_flip[...], preferred_element_type=F32)
    dhidden = dhidden * (gates[:, 2:3] + gates[:, 3:4])
    _, fwd_normed = normed_of(state, gain_ref)
    scale, bwd_normed = normed_of(saved, gain_ref)
    normed = jnp.concatenate([fwd_normed, bwd_normed], axis=0)
    both = jnp.dot(normed, cols_ref[...], preferred_element_type=F32)

    gated, upped = both[:half, :n], both[:half, n:]
    hidden = (gated * jax.nn.sigmoid(gated) * upped).astype(BF16)
    moe = jnp.dot(hidden, rows_ref[...], preferred_element_type=F32)
    new_state = state.astype(F32) + (gates[:, 0:1] + gates[:, 1:2]) * moe

    gated, upped = both[half:, :n], both[half:, n:]
    sigma = jax.nn.sigmoid(gated)
    dgate = (dhidden * upped * sigma * (1.0 + gated * (1.0 - sigma))).astype(BF16)
    dup = (dhidden * gated * sigma).astype(BF16)
    dnorm = jnp.dot(
        jnp.concatenate([dgate, dup], axis=1), cols_flip[...], preferred_element_type=F32
    )
    inner = dgate.astype(F32) * gated + dup.astype(F32) * upped
    mean = jnp.sum(inner, axis=-1, keepdims=True) / width
    value = grad.astype(F32) + scale * (gain_ref[...] * dnorm)
    put_folded(outs, 0, [new_state, value - saved.astype(F32) * (scale * scale * mean)])


def by_home_core(
    fwd_state,
    bwd_state,
    saved_input,
    fwd_route,
    bwd_route,
    fwd_gate,
    bwd_gate,
    w_gate,
    w_up,
    w_down,
    norm_gain,
):
    tokens, width = fwd_state.shape[1:]
    steps = fwd_route.shape[1]
    saved = saved_input[0].reshape(steps * tokens, width)
    small = [a.reshape(steps, tokens) for a in (fwd_route, bwd_route, fwd_gate, bwd_gate)]
    lines, *made = first_spread(small, fwd_state[0], bwd_state[0], saved)
    lines, own = lax.optimization_barrier((lines, (w_gate[0], w_up[0], w_down[0])))
    pieces = exchange(made)
    weights = pack(own)
    pair = folded(2 * width)[0]
    two = [jax.ShapeDtypeStruct((SLOT, pair), BF16)] * EXPERTS
    main = [jax.ShapeDtypeStruct((SLOT, LANES + pair), BF16)] * EXPERTS
    state = [jax.ShapeDtypeStruct((tokens, width), BF16)] * 2
    tables, later = prepare(lines, saved, steps, tokens)
    weights, tables, later = lax.optimization_barrier((weights, tables, later))
    to_tokens, to_slots, gates = tables
    for step in range(steps):
        back = call(expert_body, two, [norm_gain, *weights, *pieces])
        last = step + 1 == steps
        back = exchange(back)
        body = functools.partial(gather_body, step, last)
        made = call(body, state, [to_tokens, *back])
        if last:
            return made[0][None], made[1][None]
        made, ahead = lax.optimization_barrier((made, later[step]))
        high = swap_ranks(made[1], 1)
        low = swap_ranks(made[0], 0)
        ahead = exchange(ahead)
        args = [to_slots, gates, low, high]
        body = functools.partial(spread_body, step + 1, EXPERTS - 1)
        far = call(body, main[:1], args)
        body = functools.partial(spread_body, step + 1, 0)
        made = [*call(body, main[1:], args), *far]
        pieces = exchange(made) + ahead


def passed_along(array, axis, by):
    size = lax.axis_size(axis)
    pairs = [(i, i + by) for i in range(size) if 0 <= i + by < size]
    return lax.ppermute(array, axis, pairs)


def norm_rows(rows, gain):
    raw = rows.astype(jnp.float32)
    scale = lax.rsqrt(jnp.mean(raw * raw, axis=-1, keepdims=True) + EPS)
    return (raw, scale, (raw * scale * gain).astype(jnp.bfloat16))


def slot_index(route):
    hits = (route[:, None] == jnp.arange(EXPERTS, dtype=jnp.int32)[None, :]).astype(jnp.int32)
    before = jnp.cumsum(hits, axis=0) - hits
    return route * CAP + jnp.sum(before * hits, axis=1)


def slot_table(index):
    columns = jnp.arange(EXPERTS * CAP, dtype=jnp.int32)
    return (columns[:, None] == index[None, :]).astype(jnp.bfloat16)


def fill_slots(table, rows, shards):
    picked = jnp.dot(table, rows, preferred_element_type=jnp.float32).astype(jnp.bfloat16)
    return jnp.repeat(picked.reshape(EXPERTS, CAP, rows.shape[1]), shards, axis=0)


def collect_rows(returned, index, shards):
    width = returned.shape[2]
    summed = (
        returned.reshape(EXPERTS, shards, returned.shape[1], width).astype(jnp.float32).sum(axis=1)
    )
    return jnp.take(summed.reshape(EXPERTS * CAP, width), index, axis=0)


def by_all_to_all(
    fwd_state,
    bwd_state,
    saved_input,
    fwd_route,
    bwd_route,
    fwd_gate,
    bwd_gate,
    w_gate,
    w_up,
    w_down,
    norm_gain,
):
    shards = lax.axis_size("expert") // EXPERTS
    gain = norm_gain[0]
    gate_cols = w_gate[0]
    up_cols = w_up[0]
    down_rows = w_down[0]
    steps_total = fwd_route.shape[1]
    forward = fwd_state[0]
    backward = bwd_state[0]
    new_forward = forward
    new_backward = backward
    for moment in range(steps_total):
        fwd_index = slot_index(fwd_route[0, moment, :, 0])
        fwd_raw, _, fwd_norm = norm_rows(forward, gain)
        fwd_slots = fill_slots(slot_table(fwd_index), fwd_norm, shards)
        bwd_index = slot_index(bwd_route[0, moment, :, 0])
        bwd_table = slot_table(bwd_index)
        bwd_raw, bwd_scale, bwd_norm = norm_rows(saved_input[0, moment], gain)
        scaled = (bwd_gate[0, moment][:, None] * backward.astype(jnp.float32)).astype(jnp.bfloat16)
        bwd_inputs = fill_slots(bwd_table, bwd_norm, shards)
        bwd_grads = fill_slots(bwd_table, scaled, shards)
        expert_received = lax.all_to_all(
            fwd_slots, "expert", split_axis=0, concat_axis=0, tiled=True
        )
        expert_gated = jnp.einsum(
            "scd,dh->sch", expert_received, gate_cols, preferred_element_type=jnp.float32
        )
        expert_upped = jnp.einsum(
            "scd,dh->sch", expert_received, up_cols, preferred_element_type=jnp.float32
        )
        hidden = (expert_gated * jax.nn.sigmoid(expert_gated) * expert_upped).astype(jnp.bfloat16)
        fwd_partial = jnp.einsum(
            "sch,hd->scd", hidden, down_rows, preferred_element_type=jnp.float32
        ).astype(jnp.bfloat16)
        fwd_back = lax.all_to_all(fwd_partial, "expert", split_axis=0, concat_axis=0, tiled=True)
        inputs_part = lax.all_to_all(bwd_inputs, "expert", split_axis=0, concat_axis=0, tiled=True)
        grads_part = lax.all_to_all(bwd_grads, "expert", split_axis=0, concat_axis=0, tiled=True)
        gated = jnp.einsum(
            "scd,dh->sch", inputs_part, gate_cols, preferred_element_type=jnp.float32
        )
        upped = jnp.einsum("scd,dh->sch", inputs_part, up_cols, preferred_element_type=jnp.float32)
        dhidden = jnp.einsum(
            "scd,hd->sch", grads_part, down_rows, preferred_element_type=jnp.float32
        )
        sigma = jax.nn.sigmoid(gated)
        dgate = (dhidden * upped * sigma * (1.0 + gated * (1.0 - sigma))).astype(jnp.bfloat16)
        dup = (dhidden * gated * sigma).astype(jnp.bfloat16)
        result = jnp.einsum("sch,dh->scd", dgate, gate_cols, preferred_element_type=jnp.float32)
        result = result + jnp.einsum(
            "sch,dh->scd", dup, up_cols, preferred_element_type=jnp.float32
        )
        bwd_partial = result.astype(jnp.bfloat16)
        bwd_back = lax.all_to_all(bwd_partial, "expert", split_axis=0, concat_axis=0, tiled=True)
        moe_rows = collect_rows(fwd_back, fwd_index, shards)
        new_forward = (fwd_raw + fwd_gate[0, moment][:, None] * moe_rows).astype(jnp.bfloat16)
        dnorm = collect_rows(bwd_back, bwd_index, shards)
        weighted = gain * dnorm
        cubed = bwd_scale * bwd_scale * bwd_scale
        dinput = bwd_scale * weighted - bwd_raw * cubed * jnp.mean(
            bwd_raw * weighted, axis=-1, keepdims=True
        )
        new_backward = (backward.astype(jnp.float32) + dinput).astype(jnp.bfloat16)
        if moment + 1 < steps_total:
            forward = passed_along(new_forward, "pipe", 1)
            backward = passed_along(new_backward, "pipe", -1)
    return (new_forward[None], new_backward[None])


def local(*args):
    if lax.axis_size("expert") == 2 * EXPERTS:
        return by_home_core(*args)
    return by_all_to_all(*args)


def solution(mesh):
    specs = (
        P("pipe", "expert", None),
        P("pipe", "expert", None),
        P("pipe", None, "expert", None),
        P("pipe", None, "expert", None),
        P("pipe", None, "expert", None),
        P("pipe", None, "expert"),
        P("pipe", None, "expert"),
        P("pipe", None, "expert"),
        P("pipe", None, "expert"),
        P("pipe", "expert", None),
        P("pipe", None),
    )
    return jax.shard_map(
        local,
        mesh=mesh,
        in_specs=specs,
        out_specs=(P("pipe", "expert", None), P("pipe", "expert", None)),
        check_vma=False,
    )
```
